32 devices in a mesh: grp: 2 (over x), tok: 8 (over z, y), wid: 2 (over core).
Axes of the slice: x: 2, y: 2, z: 4, core: 2. Of those that a mesh axis runs over, the one named last changes fastest.
Arguments:
- inputs: bfloat16 [128, 8192], P(('grp', 'wid'), 'tok'), may hold values from -6 to 6
- parent_gate: bfloat16 [8192, 28672], P('tok', ('grp', 'wid')), may hold values from -0.0625 to 0.0625
- parent_up: bfloat16 [8192, 28672], P('tok', ('grp', 'wid')), may hold values from -0.0625 to 0.0625
- parent_down: bfloat16 [28672, 8192], P(('grp', 'wid'), 'tok'), may hold values from -0.03125 to 0.03125
- first_gate: bfloat16 [8192, 7168], P('tok', ('grp', 'wid')), may hold values from -0.0625 to 0.0625
- first_up: bfloat16 [8192, 7168], P('tok', ('grp', 'wid')), may hold values from -0.0625 to 0.0625
- first_down: bfloat16 [7168, 8192], P(('grp', 'wid'), 'tok'), may hold values from -0.0625 to 0.0625
- second_gate: bfloat16 [8192, 5632], P('tok', ('grp', 'wid')), may hold values from -0.0625 to 0.0625
- second_up: bfloat16 [8192, 5632], P('tok', ('grp', 'wid')), may hold values from -0.0625 to 0.0625
- second_down: bfloat16 [5632, 8192], P(('grp', 'wid'), 'tok'), may hold values from -0.078125 to 0.078125
Outputs:
- target: bfloat16 [128, 8192], P(('grp', 'wid'), 'tok')
- first_error: bfloat16 [128, 8192], P(('grp', 'wid'), 'tok')
- second_error: bfloat16 [128, 8192], P(('grp', 'wid'), 'tok')
- first_grad_gate: bfloat16 [8192, 7168], P('tok', ('grp', 'wid'))
- first_grad_up: bfloat16 [8192, 7168], P('tok', ('grp', 'wid'))
- first_grad_down: bfloat16 [7168, 8192], P(('grp', 'wid'), 'tok')
- second_grad_gate: bfloat16 [8192, 5632], P('tok', ('grp', 'wid'))
- second_grad_up: bfloat16 [8192, 5632], P('tok', ('grp', 'wid'))
- second_grad_down: bfloat16 [5632, 8192], P(('grp', 'wid'), 'tok')
The draws below stay inside these ranges and needn't reach their ends.
All inputs are finite; a program needn't handle non-finite values.
Results may differ from the reference program's by a relative error of at most 0.009.
Values may be sent and summed in bfloat16 or wider, within the bound.
A program may use at most 192 MiB of HBM per device.

```python
import jax
import jax.numpy as jnp
from jax import lax

D = 8192
FF = 28672
HA = 7168
HB = 5632
TOKENS = 128


def level_of(rng, extent, shards, low, top_value):
    factor_of = 1.0
    for axis_at, shards_of in shards:
        steps = jax.random.uniform(jax.random.fold_in(jax.random.fold_in(rng, 6), axis_at), (shards_of,), jnp.float32, low / len(shards), top_value / len(shards))
        factor_of = factor_of * jnp.repeat(jnp.exp(steps), extent[axis_at] // shards_of).reshape((-1,) + (1,) * (len(extent) - 1 - axis_at))
    return factor_of


def normal_values(own_key, extent, width, limit, pieces=(), kind=jnp.bfloat16):
    drawn = jax.random.normal(own_key, extent, jnp.float32) * width
    if len(pieces) > 0:
        drawn = level_of(own_key, extent, pieces, -0.22, 0.18) * drawn
    return jnp.clip(drawn, min=-limit, max=limit).astype(kind)


def setup_inputs(seed: int = 0) -> dict:
    arg_keys = jax.random.split(jax.random.key(seed), 11)
    inputs = normal_values(arg_keys[0], (TOKENS, D), 1.0, 6.0, ((0, 4), (1, 8)))
    parent_gate = normal_values(arg_keys[1], (D, FF), D ** -0.5, 0.0625, ((0, 8), (1, 4)))
    parent_up = normal_values(arg_keys[2], (D, FF), D ** -0.5, 0.0625, ((0, 8), (1, 4)))
    parent_down = normal_values(arg_keys[3], (FF, D), FF ** -0.5, 0.03125, ((0, 4), (1, 8)))
    first_gate = normal_values(arg_keys[4], (D, HA), D ** -0.5, 0.0625, ((0, 8), (1, 4)))
    first_up = normal_values(arg_keys[5], (D, HA), D ** -0.5, 0.0625, ((0, 8), (1, 4)))
    first_down = normal_values(arg_keys[6], (HA, D), HA ** -0.5, 0.0625, ((0, 4), (1, 8)))
    second_gate = normal_values(arg_keys[7], (D, HB), D ** -0.5, 0.0625, ((0, 8), (1, 4)))
    second_up = normal_values(arg_keys[8], (D, HB), D ** -0.5, 0.0625, ((0, 8), (1, 4)))
    second_down = normal_values(arg_keys[9], (HB, D), HB ** -0.5, 0.078125, ((0, 4), (1, 8)))
    return dict(inputs=inputs, parent_gate=parent_gate, parent_up=parent_up, parent_down=parent_down, first_gate=first_gate, first_up=first_up, first_down=first_down, second_gate=second_gate, second_up=second_up, second_down=second_down)


def matmul(left, right):
    return jnp.dot(left, right, preferred_element_type=jnp.float32)


def inner_rows(left, right):
    return lax.dot_general(left, right, (((0,), (0,)), ((), ())), preferred_element_type=jnp.float32)


def outer_cols(left, right):
    return lax.dot_general(left, right, (((1,), (1,)), ((), ())), preferred_element_type=jnp.float32)


def candidate_pass(inputs, target, gate_w, up_w, down_w):
    pre_gate = matmul(inputs, gate_w)
    pre_up = matmul(inputs, up_w)
    hidden = (jax.nn.silu(pre_gate) * pre_up).astype(jnp.bfloat16)
    output_full = matmul(hidden, down_w)
    error_vals = (output_full - target.astype(jnp.float32)).astype(jnp.bfloat16)
    grad_down = inner_rows(hidden, error_vals).astype(jnp.bfloat16)
    back_grad = outer_cols(error_vals, down_w)
    sigmoid_gate = jax.nn.sigmoid(pre_gate)
    grad_pre_gate = (back_grad * pre_up * sigmoid_gate * (1.0 + pre_gate * (1.0 - sigmoid_gate))).astype(jnp.bfloat16)
    grad_pre_up = (back_grad * pre_gate * sigmoid_gate).astype(jnp.bfloat16)
    grad_gate = inner_rows(inputs, grad_pre_gate).astype(jnp.bfloat16)
    grad_up = inner_rows(inputs, grad_pre_up).astype(jnp.bfloat16)
    return error_vals, grad_gate, grad_up, grad_down


def reference(inputs, parent_gate, parent_up, parent_down, first_gate, first_up, first_down, second_gate, second_up, second_down):
    parent_pre_gate = matmul(inputs, parent_gate)
    parent_pre_up = matmul(inputs, parent_up)
    parent_hidden = (jax.nn.silu(parent_pre_gate) * parent_pre_up).astype(jnp.bfloat16)
    target = matmul(parent_hidden, parent_down).astype(jnp.bfloat16)
    first_error, first_grad_gate, first_grad_up, first_grad_down = candidate_pass(inputs, target, first_gate, first_up, first_down)
    second_error, second_grad_gate, second_grad_up, second_grad_down = candidate_pass(inputs, target, second_gate, second_up, second_down)
    return (target, first_error, second_error, first_grad_gate, first_grad_up, first_grad_down, second_grad_gate, second_grad_up, second_grad_down)
```

```python
import functools

import jax
import jax.numpy as jnp
from jax import lax
from jax.experimental import pallas as pl
from jax.experimental.pallas import tpu as pltpu
from jax.sharding import PartitionSpec as P

MESH = pl.DeviceIdType.MESH
LANES = 128
MIB = 1024 * 1024
SLOTS = 4
FORWARD_STEPS = (2, 2, 2, 1, 2, 2, 2)
BACKWARD_STEPS = (3, 3, 3, 3, 4, 3, 2)
FORWARD_MIB = 48
F32 = jnp.float32
BF16 = jnp.bfloat16


def matmul(left, right):
    return jnp.dot(left, right, preferred_element_type=F32)


def inner_rows(left, right):
    return lax.dot_general(left, right, (((0,), (0,)), ((), ())), preferred_element_type=F32)


def outer_cols(left, right):
    return lax.dot_general(left, right, (((1,), (1,)), ((), ())), preferred_element_type=F32)


def remote(src, dst, send, recv, where):
    return pltpu.make_async_remote_copy(
        src_ref=src, dst_ref=dst, send_sem=send, recv_sem=recv,
        device_id=where, device_id_type=MESH,
    )


def divisor(total, most):
    return max(k for k in range(1, most + 1) if total % k == 0)


def relay(dims, steps, produce, finish, consume, partial, out, span, bufs, sems, prepare):
    na, nb, jobs, slots = dims
    side = nb - 1
    ay_out, ay_in, az_out, az_in, bz_out, bz_in, by_out, by_in = bufs
    (say, ray, saz, raz, sbz, rbz, sby, rby,
     tay, uay, taz, uaz, tbz, ubz, tby, uby) = sems

    me = lax.axis_index("tok")
    hi, lo = me // nb, lax.rem(me, nb)
    peers = [lax.rem(lo + d, nb) for d in range(1, nb)]
    beside = [{"tok": hi * nb + p} for p in peers]
    pos = [hi, na - 1 - hi]
    far = [na - 1 - p for p in pos]
    onward = [
        {"tok": lax.rem(hi + 1, na) * nb + lo}, {"tok": lax.rem(hi + na - 1, na) * nb + lo}
    ]
    back = onward[::-1]
    end = (hi == 0) | (hi == na - 1)
    turn = jnp.where(hi == na - 1, 0, 1)

    barrier = pltpu.get_barrier_semaphore()
    for where in beside:
        pl.semaphore_signal(barrier, inc=1, device_id=where, device_id_type=MESH)
    for d in range(2):
        @pl.when(pos[d] < na - 1)
        def _(d=d):
            pl.semaphore_signal(barrier, inc=1, device_id=onward[d], device_id_type=MESH)
    prepare(barrier, side + jnp.where(end, 1, 2))

    def a_block(y, d):
        return y * 2 + d

    def b_block(y, d):
        return 2 * nb + d * nb + y

    def piece(block, j, count=1):
        return out.at[pl.ds(block, count), :, pl.ds(pl.multiple_of(j * span, LANES), span)]

    def copy_ay(j, k):
        return remote(ay_out.at[j, k], ay_in.at[j, k], say.at[j, k], ray.at[j, k], beside[k])

    def copy_az(j, d):
        return remote(az_out.at[j, d], az_in.at[j, d], saz.at[j, d], raz.at[j, d], onward[d])

    def copy_bz(j, d):
        return remote(bz_out.at[j, d], bz_in.at[j, d], sbz.at[j, d], rbz.at[j, d], onward[d])

    def copy_by(j, k):
        return remote(by_out.at[j, k], by_in.at[j, k], sby.at[j, k], rby.at[j, k], beside[k])

    def spread_az(j, d):
        here = piece(a_block(lo, d), j)
        return remote(here, here, taz.at[j, d], uaz.at[j, d], back[d])

    def spread_ay(j, d, k):
        here = piece(a_block(lo, d), j)
        return remote(here, here, tay.at[j, d, k], uay.at[j, d, k], beside[k])

    def spread_by(j, k):
        here = piece(b_block(lo, turn), j)
        return remote(here, here, tby.at[j, k], uby.at[j, k], beside[k])

    def spread_bz(j, d):
        here = piece(b_block(0, d), j, nb)
        return remote(here, here, tbz.at[j, d], ubz.at[j, d], back[d])

    def on(j, condition=None):
        inside = (j >= 0) & (j < jobs)
        return pl.when(inside if condition is None else inside & condition)

    def begin(j):
        slot = lax.rem(j, slots)
        produce(j, slot)
        for k in range(side):
            ay_out[j, k] = partial[slot, pl.ds(peers[k] * 2, 2)].astype(BF16)
            copy_ay(j, k).start()
        for d in range(2):
            @pl.when(pos[d] == 0)
            def _(d=d):
                bz_out[j, d] = partial[slot, pl.ds(b_block(0, d), nb)].astype(BF16)
                copy_bz(j, d).start()

    def pair(j):
        slot = lax.rem(j, slots)
        for k in range(side):
            copy_ay(j, k).wait_recv()
        for d in range(2):
            total = partial[slot, a_block(lo, d)]
            for k in range(side):
                total = total + ay_in[j, k, d].astype(F32)
            partial[slot, a_block(lo, d)] = total

            @pl.when(pos[d] == 0)
            def _(d=d, total=total):
                az_out[j, d] = total.astype(BF16)
                copy_az(j, d).start()

    def along_a(j, d):
        slot = lax.rem(j, slots)
        copy_az(j, d).wait_recv()
        total = partial[slot, a_block(lo, d)] + az_in[j, d].astype(F32)

        @pl.when(pos[d] < na - 1)
        def _():
            az_out[j, d] = total.astype(BF16)
            copy_az(j, d).start()

        @pl.when(pos[d] == na - 1)
        def _():
            finish(j, 0, a_block(lo, d), total)
            spread_az(j, d).start()
            for k in range(side):
                spread_ay(j, d, k).start()

    def along_b(j, d):
        slot = lax.rem(j, slots)
        copy_bz(j, d).wait_recv()

        @pl.when(pos[d] < na - 1)
        def _():
            for y in range(nb):
                total = partial[slot, b_block(y, d)] + bz_in[j, d, y].astype(F32)
                bz_out[j, d, y] = total.astype(BF16)
            copy_bz(j, d).start()

        @pl.when(pos[d] == na - 1)
        def _():
            for k in range(side):
                total = partial[slot, b_block(peers[k], d)]
                total = total + bz_in[j, d, peers[k]].astype(F32)
                by_out[j, k] = total.astype(BF16)
                copy_by(j, k).start()
            total = partial[slot, b_block(lo, d)] + bz_in[j, d, lo].astype(F32)
            partial[slot, b_block(lo, d)] = total

    def corner(j):
        slot = lax.rem(j, slots)
        block = b_block(lo, turn)
        total = partial[slot, block]
        for k in range(side):
            copy_by(j, k).wait_recv()
            total = total + by_in[j, k].astype(F32)
        finish(j, 1, block, total)
        for k in range(side):
            spread_by(j, k).start()

    def leave_b(j):
        for k in range(side):
            spread_by(j, k).wait_recv()
        for d in range(2):
            @pl.when(pos[d] == na - 1)
            def _(d=d):
                spread_bz(j, d).start()

    def pass_a(j, d):
        spread_az(j, d).wait_recv()

        @pl.when(far[d] < na - 1)
        def _():
            spread_az(j, d).start()

        for k in range(side):
            spread_ay(j, d, k).start()

    def pass_b(j, d):
        spread_bz(j, d).wait_recv()

        @pl.when(far[d] < na - 1)
        def _():
            spread_bz(j, d).start()

    start_a, walk_a, walk_b, turn_b, turn_c, open_a, open_b = steps
    top = start_a + walk_a * (na - 1)
    turn_at = walk_b * (na - 1) + turn_b
    leave_at = turn_at + turn_c
    done = 1 + max(top + open_a * na, leave_at + open_b * (na - 1))

    def tick(t, carry):
        on(t)(functools.partial(begin, t))
        j = t - start_a
        on(j)(functools.partial(pair, j))
        for d in range(2):
            j = t - walk_b * pos[d]
            on(j, pos[d] > 0)(functools.partial(along_b, j, d))
        for d in range(2):
            j = t - start_a - walk_a * pos[d]
            on(j, pos[d] > 0)(functools.partial(along_a, j, d))
        j = t - turn_at
        on(j, end)(functools.partial(corner, j))
        j = t - leave_at
        on(j, end)(functools.partial(leave_b, j))
        for d in range(2):
            j = t - top - open_a * far[d]
            on(j, far[d] > 0)(functools.partial(pass_a, j, d))
        for d in range(2):
            j = t - leave_at - open_b * far[d]
            on(j, far[d] > 0)(functools.partial(pass_b, j, d))
        j = t - done
        on(j)(functools.partial(arrive, j))
        return carry

    def arrive(j):
        for k in range(side):
            for d in range(2):
                spread_ay(j, d, k).wait_recv()
        consume(j)

    lax.fori_loop(0, jobs + done, tick, 0)

    def drain(j, carry):
        for k in range(side):
            copy_ay(j, k).wait_send()
            for d in range(2):
                spread_ay(j, d, k).wait_send()
        for d in range(2):
            @pl.when(pos[d] < na - 1)
            def _(d=d):
                copy_az(j, d).wait_send()
                copy_bz(j, d).wait_send()

            @pl.when(far[d] < na - 1)
            def _(d=d):
                spread_az(j, d).wait_send()
                spread_bz(j, d).wait_send()

        @pl.when(end)
        def _():
            for k in range(side):
                copy_by(j, k).wait_send()
                spread_by(j, k).wait_send()

        return carry

    return lambda: lax.fori_loop(0, jobs, drain, 0)


def relay_scratch(dims, rows, width):
    na, nb, jobs, slots = dims
    side = max(nb - 1, 1)
    dma = pltpu.SemaphoreType.DMA

    def room(*shape):
        return pltpu.VMEM((jobs,) + shape + (rows, width), BF16)

    bufs = [
        room(side, 2), room(side, 2), room(2), room(2),
        room(2, nb), room(2, nb), room(side), room(side),
    ]
    counts = [(side,), (2,), (2,), (side,), (2, side), (2,), (2,), (side,)]
    sems = [dma((jobs,) + c) for c in counts for _ in range(2)]
    partial = pltpu.VMEM((slots, 4 * nb, rows, width), F32)
    return [partial] + bufs + sems


def ring_slots(na, steps):
    return 1 + max(steps[0] + steps[1] * (na - 1), steps[2] * (na - 1) + steps[3])


def layout_of(tok, tokens):
    na = 4 if tok % 4 == 0 else tok
    nb = tok // na
    return na, nb, tokens // (4 * nb)


def plane(sizes):
    ngrp, nwid = sizes
    g, w = lax.axis_index("grp"), lax.axis_index("wid")
    spots = [
        ((d, e), lax.rem(g + d, ngrp), lax.rem(w + e, nwid))
        for d in range(ngrp) for e in range(nwid) if d or e
    ]
    return g * nwid + w, [(step, p * nwid + q, {"grp": p, "wid": q}) for step, p, q in spots]


def spreader(sizes, view, mine, sems):
    ngrp, nwid = sizes
    send, recv = sems
    g, w = lax.axis_index("grp"), lax.axis_index("wid")

    def copy(d, e, block, source=None):
        n = d * nwid + e - 1
        if e == 0:
            where = {"grp": lax.rem(g + d, ngrp)}
        else:
            where = {"wid": lax.rem(w + e, nwid)}
        here = view(block)
        return remote(here if source is None else source, here, send.at[n], recv.at[n], where)

    direct = [(d, 0) for d in range(1, ngrp)] + [(0, e) for e in range(1, nwid)]
    handed = [(d, e) for d in range(1, ngrp) for e in range(1, nwid)]

    def origin(d):
        return lax.rem(g + ngrp - d, ngrp) * nwid + w

    def first():
        for d, e in direct:
            copy(d, e, g * nwid + w, mine).start()

    def second():
        for d in range(1, ngrp):
            copy(d, 0, g * nwid + w).wait_recv()
        for d, e in handed:
            copy(d, e, origin(d)).start()

    def last():
        for e in range(1, nwid):
            copy(0, e, g * nwid + w).wait_recv()
        for d, e in handed:
            copy(d, e, origin(d)).wait_recv()

    def close():
        for d, e in direct + handed:
            copy(d, e, g * nwid + w).wait_send()

    return first, second, last, close


def forward_kernel(dims, counts, group, sizes, *refs):
    na, nb, jobs, slots = dims
    many = len(counts)
    x_ref = refs[0]
    weights = [refs[1 + 2 * i: 3 + 2 * i] for i in range(many)]
    downs = refs[1 + 2 * many: 1 + 3 * many]
    (
        x, out, kept, target, own, full, near,
        held, loaded, below, lowered, stored, total_of, shares, got,
        sx, rx, ss, rs, se, re, partial,
    ) = refs[1 + 3 * many: 23 + 3 * many]
    rest = refs[23 + 3 * many:]
    bufs, sems = rest[:8], rest[8:]
    starts = [sum(counts[:i]) for i in range(many + 1)]
    rows = out.shape[1]
    kept_jobs = kept.shape[2] // (2 * LANES * group)
    near_units = starts[many - 1]
    near_job = (near_units - 1) // group
    members, height, features = full.shape[1:]
    pieces = ss.shape[0]
    step = features // pieces
    me, places = plane(sizes)

    def fetch(ref, column, slot, u, i):
        return pltpu.make_async_copy(
            ref.at[:, pl.ds(pl.multiple_of(column, LANES), LANES)],
            held.at[slot, u, :, pl.ds(i * LANES, LANES)],
            loaded.at[slot, u, i],
        )

    def load(j):
        slot = lax.rem(j, SLOTS)
        for u in range(group):
            c = j * group + u
            for n, pair in enumerate(weights):
                @pl.when((c >= starts[n]) & (c < starts[n + 1]))
                def _(u=u, c=c, n=n, pair=pair):
                    for i in range(2):
                        fetch(pair[i], (c - starts[n]) * LANES, slot, u, i).start()

    def below_copy(c):
        slot = lax.rem(c, below.shape[0])
        row = pl.multiple_of((c - near_units) * LANES, LANES)
        return pltpu.make_async_copy(
            downs[many - 1].at[pl.ds(row, LANES), :], below.at[slot], lowered.at[slot]
        )

    def near_copy(n):
        height_n = counts[n] * LANES
        return pltpu.make_async_copy(
            downs[n], near.at[pl.ds(starts[n] * LANES, height_n), :], stored.at[n]
        )

    xs = spreader(sizes, lambda block: x.at[block], x_ref, (sx, rx))

    def share(n, p, k, block, where):
        cols = pl.ds(p * step, step)
        return remote(
            shares.at[n, block, :, cols], got.at[k, n, :, cols],
            ss.at[p, n, k], rs.at[p, n, k], where,
        )

    def give(n):
        for p in range(pieces):
            cols = pl.ds(p * step, step)
            shares[n, :, :, cols] = total_of[n, :, cols].astype(BF16).reshape(
                members, height, step
            )
            for k, (_, block, where) in enumerate(places):
                share(n, p, k, block, where).start()

    def prepare(barrier, count):
        for _, _, where in places:
            pl.semaphore_signal(barrier, inc=1, device_id=where, device_id_type=MESH)
        for j in range(min(SLOTS, jobs)):
            load(j)
        for n in range(many - 1):
            near_copy(n).start()
        for c in range(near_units, min(near_units + below.shape[0], starts[-1])):
            below_copy(c).start()
        total_of[...] = jnp.zeros_like(total_of)
        x[me] = x_ref[...]
        pl.semaphore_wait(barrier, count + len(places))
        xs[0]()
        xs[1]()
        xs[2]()

    def produce(j, part):
        slot = lax.rem(j, SLOTS)
        left = x[...].reshape(members * height, features)
        for u in range(group):
            for i in range(2):
                fetch(weights[0][0], 0, slot, u, i).wait()
            product = matmul(left, held[slot, u])
            partial[part, :, :, pl.ds(u * 2 * LANES, 2 * LANES)] = product.reshape(
                4 * nb, rows, 2 * LANES
            )

        @pl.when(j + SLOTS < jobs)
        def _():
            load(j + SLOTS)

    def finish(j, kind, block, total):
        for u in range(group):
            gate = total[:, u * 2 * LANES: u * 2 * LANES + LANES]
            up = total[:, u * 2 * LANES + LANES: (u + 1) * 2 * LANES]
            column = pl.multiple_of((j * group + u) * LANES, LANES)
            out[block, :, pl.ds(column, LANES)] = (
                gate / (1.0 + jnp.exp(-gate)) * up
            ).astype(BF16)

        @pl.when(j < kept_jobs)
        def _():
            wide = 2 * LANES * group
            kept[kind, :, pl.ds(pl.multiple_of(j * wide, LANES), wide)] = total

    def consume(j):
        for u in range(group):
            c = j * group + u
            column = pl.multiple_of(c * LANES, LANES)
            left = out[:, :, pl.ds(column, LANES)].reshape(members * height, LANES)
            for n in range(many - 1):
                @pl.when((c >= starts[n]) & (c < starts[n + 1]))
                def _(n=n, c=c, column=column, left=left):
                    pl.when(c == starts[n])(lambda: near_copy(n).wait())
                    total_of[n] += matmul(left, near[pl.ds(column, LANES), :])

            @pl.when(c >= near_units)
            def _(c=c, left=left):
                slot = lax.rem(c, below.shape[0])
                below_copy(c).wait()
                total_of[many - 1] += matmul(left, below[slot])

                @pl.when(c + below.shape[0] < starts[-1])
                def _():
                    below_copy(c + below.shape[0]).start()

        @pl.when(j == near_job)
        def _():
            for n in range(many - 1):
                give(n)

    close = relay(
        dims, FORWARD_STEPS, produce, finish, consume, partial, out, group * LANES, bufs,
        sems, prepare,
    )

    give(many - 1)
    spreads = []
    for p in range(pieces):
        cols = pl.ds(p * step, step)
        sums = []
        for n in range(many):
            total = shares[n, me, :, cols].astype(F32)
            for k, (_, block, where) in enumerate(places):
                share(n, p, k, block, where).wait_recv()
                total = total + got[k, n, :, cols].astype(F32)
            sums.append(total)
        goal = sums[-1].astype(BF16)
        target[:, cols] = goal
        goal = goal.astype(F32)
        for n in range(many - 1):
            value = (sums[n] - goal).astype(BF16)
            own[n, :, cols] = value
            full[n, me, :, cols] = value
        spread = spreader(
            sizes, lambda block, cols=cols: full.at[:, block, :, cols], own.at[:, :, cols],
            (se.at[p], re.at[p]),
        )
        spread[0]()
        spreads.append(spread)
    for spread in spreads:
        spread[1]()
    for spread in spreads:
        spread[2]()
    for spread in spreads + [xs]:
        spread[3]()
    for n in range(many):
        for p in range(pieces):
            for k, (_, block, where) in enumerate(places):
                share(n, p, k, block, where).wait_send()
    close()


def forward(inputs, weights, downs, tok, sizes):
    height, features = inputs.shape
    members = sizes[0] * sizes[1]
    tokens = members * height
    na, nb, rows = layout_of(tok, tokens)
    weights = [padded(w) for w in weights]
    downs = [jnp.pad(d, ((0, -d.shape[0] % LANES), (0, 0))) for d in downs]
    counts = [w.shape[1] // LANES for w in weights[::2]]
    many = len(counts)
    group = divisor(sum(counts), 3)
    jobs = sum(counts) // group
    dims = (na, nb, jobs, ring_slots(na, FORWARD_STEPS))
    kept_jobs = -(-(sum(counts[:-1]) + 1) // group)
    width = 2 * LANES * group
    pieces = max(features // 256, 1)
    vmem = pl.BlockSpec(memory_space=pltpu.VMEM)
    hbm = pl.BlockSpec(memory_space=pltpu.HBM)
    dma = pltpu.SemaphoreType.DMA
    shape = jax.ShapeDtypeStruct
    lower = 2 * group
    outs = pl.pallas_call(
        functools.partial(forward_kernel, dims, counts, group, sizes),
        out_shape=[
            shape((members, height, features), BF16),
            shape((4 * nb, rows, sum(counts) * LANES), BF16),
            shape((2, rows, kept_jobs * width), F32),
            shape((height, features), BF16),
            shape((many - 1, height, features), BF16),
            shape((many - 1, members, height, features), BF16),
        ],
        in_specs=[vmem] + [hbm] * (3 * many),
        out_specs=[vmem] * 6,
        scratch_shapes=[
            pltpu.VMEM((sum(counts[:-1]) * LANES, features), BF16),
            pltpu.VMEM((SLOTS, group, features, 2 * LANES), BF16), dma((SLOTS, group, 2)),
            pltpu.VMEM((lower, LANES, features), BF16), dma((lower,)), dma((many - 1,)),
            pltpu.VMEM((many, tokens, features), F32),
            pltpu.VMEM((many, members, height, features), BF16),
            pltpu.VMEM((members - 1, many, height, features), BF16),
            dma((members - 1,)), dma((members - 1,)),
            dma((pieces, many, members - 1)), dma((pieces, many, members - 1)),
            dma((pieces, members - 1)), dma((pieces, members - 1)),
        ] + relay_scratch(dims, rows, width),
        compiler_params=pltpu.CompilerParams(
            collective_id=2, has_side_effects=True, vmem_limit_bytes=FORWARD_MIB * MIB
        ),
        name="forward_exchange",
    )(inputs, *weights, *downs)
    return outs, counts, downs[:-1]


def backward_kernel(dims, counts, group, full, kept, *rest):
    na, nb, jobs, slots = dims
    many = len(counts)
    downs = rest[:many]
    out, near, stored, partial = rest[many: many + 4]
    bufs, sems = rest[many + 4: many + 12], rest[many + 12:]
    starts = [sum(counts[:i]) for i in range(many + 1)]
    rows = out.shape[1]
    features = full.shape[3]

    def near_copy(n, u, c):
        return pltpu.make_async_copy(
            downs[n].at[pl.ds(u * LANES, LANES), :],
            near.at[pl.ds(pl.multiple_of(c * LANES, LANES), LANES), :], stored.at[c],
        )

    def produce(j, part):
        for u in range(group):
            c = j * group + u
            for n in range(many):
                @pl.when((c >= starts[n]) & (c < starts[n + 1]))
                def _(u=u, c=c, n=n):
                    error = full[n].reshape(4 * nb * rows, features)
                    row = pl.multiple_of(c * LANES, LANES)
                    near_copy(n, 0, c).wait()
                    product = outer_cols(error, near[pl.ds(row, LANES), :])
                    partial[part, :, :, pl.ds(u * LANES, LANES)] = product.reshape(
                        4 * nb, rows, LANES
                    )

            @pl.when(c >= starts[many])
            def _(u=u):
                partial[part, :, :, pl.ds(u * LANES, LANES)] = jnp.zeros(
                    (4 * nb, rows, LANES), F32
                )

    def finish(j, kind, block, total):
        for u in range(group):
            column = pl.multiple_of((j * group + u) * 2 * LANES, LANES)
            gate = kept[kind, :, pl.ds(column, LANES)]
            up = kept[kind, :, pl.ds(column + LANES, LANES)]
            value = total[:, u * LANES: (u + 1) * LANES]
            s = 1.0 / (1.0 + jnp.exp(-gate))
            out[block, :, pl.ds(column, LANES)] = (
                value * up * s * (1.0 + gate * (1.0 - s))
            ).astype(BF16)
            out[block, :, pl.ds(column + LANES, LANES)] = (value * gate * s).astype(BF16)

    def prepare(barrier, count):
        for n in range(many):
            for u in range(counts[n]):
                near_copy(n, u, starts[n] + u).start()
        pl.semaphore_wait(barrier, count)

    relay(
        dims, BACKWARD_STEPS, produce, finish, lambda j: None, partial, out,
        group * 2 * LANES, bufs, sems, prepare,
    )()


def backward(full, downs, kept, counts, tok):
    tokens = full.shape[1] * full.shape[2]
    na, nb, rows = layout_of(tok, tokens)
    group = 2
    jobs = -(-sum(counts) // group)
    dims = (na, nb, jobs, ring_slots(na, BACKWARD_STEPS))
    vmem = pl.BlockSpec(memory_space=pltpu.VMEM)
    grads = pl.pallas_call(
        functools.partial(backward_kernel, dims, counts, group),
        out_shape=jax.ShapeDtypeStruct((4 * nb, rows, jobs * group * 2 * LANES), BF16),
        in_specs=[vmem] * 2 + [pl.BlockSpec(memory_space=pltpu.HBM)] * len(downs),
        out_specs=vmem,
        scratch_shapes=[
            pltpu.VMEM((sum(counts) * LANES, full.shape[3]), BF16),
            pltpu.SemaphoreType.DMA((sum(counts),)),
        ] + relay_scratch(dims, rows, group * LANES),
        compiler_params=pltpu.CompilerParams(
            collective_id=3, has_side_effects=True, vmem_limit_bytes=20 * MIB
        ),
        name="backward_exchange",
    )(full, kept, *downs)
    return grads.reshape(tokens, jobs * group * 2 * LANES)


def padded(x):
    return jnp.pad(x, ((0, 0), (0, -x.shape[1] % LANES)))


def outer_kernel(counts, columns, grads, hidden, full, target, own, *outs):
    many = len(counts)
    tokens = columns.shape[0]
    outs[0][...] = target[...]
    for n in range(many):
        outs[1 + n][...] = own[n]
    downs = outs[1 + many: 1 + 2 * many]
    sides = outs[1 + 2 * many:]
    left = columns[...].T
    c = 0
    for n, count in enumerate(counts):
        gate, up = sides[2 * n], sides[2 * n + 1]
        error = full[n].reshape(tokens, full.shape[3])
        height = downs[n].shape[0]
        at = c * LANES
        downs[n][...] = inner_rows(hidden[:, at: at + height], error).astype(BF16)
        for u in range(count):
            product = matmul(left, grads[:, c * 2 * LANES: (c + 1) * 2 * LANES]).astype(BF16)
            size = min(LANES, gate.shape[1] - u * LANES)
            gate[:, u * LANES: u * LANES + size] = product[:, :size]
            up[:, u * LANES: u * LANES + size] = product[:, LANES: LANES + size]
            c += 1


def weight_grads(columns, grads, hidden, full, target, own, counts, widths):
    tokens, features = columns.shape
    tile = LANES
    many, members, height = full.shape[:3]
    out_bytes = 6 * features * sum(widths)
    sides = [w for w in widths for _ in range(2)]
    shape = jax.ShapeDtypeStruct
    whole = pl.BlockSpec(memory_space=pltpu.VMEM)
    lane = pl.BlockSpec((height, tile), lambda i: (0, i))
    return pl.pallas_call(
        functools.partial(outer_kernel, counts),
        grid=(features // tile,),
        out_shape=[shape((height, features), BF16)] * (1 + many)
        + [shape((w, features), BF16) for w in widths]
        + [shape((features, w), BF16) for w in sides],
        in_specs=[
            pl.BlockSpec((tokens, tile), lambda i: (0, i)), whole, whole,
            pl.BlockSpec((many, members, height, tile), lambda i: (0, 0, 0, i)),
            lane, pl.BlockSpec((many, height, tile), lambda i: (0, 0, i)),
        ],
        out_specs=[lane] * (1 + many)
        + [pl.BlockSpec((w, tile), lambda i: (0, i)) for w in widths]
        + [pl.BlockSpec((tile, w), lambda i: (i, 0)) for w in sides],
        compiler_params=pltpu.CompilerParams(vmem_limit_bytes=24 * MIB),
        cost_estimate=pl.CostEstimate(
            flops=tokens * out_bytes, bytes_accessed=out_bytes, transcendentals=0
        ),
        name="weight_grads",
    )(columns, grads, hidden, full, target, own)


def body(
    tok, sizes, inputs, parent_gate, parent_up, parent_down, first_gate, first_up, first_down,
    second_gate, second_up, second_down,
):
    weights = (first_gate, first_up, second_gate, second_up, parent_gate, parent_up)
    downs = (first_down, second_down, parent_down)
    (x, hidden, kept, target, own, full), counts, nearest = forward(
        inputs, weights, downs, tok, sizes
    )
    tokens = x.shape[0] * x.shape[1]
    counts = counts[:-1]
    grads = backward(full, nearest, kept, counts, tok)
    near_hidden = hidden.reshape(tokens, -1)
    (
        target, first_error, second_error, first_grad_down, second_grad_down,
        first_grad_gate, first_grad_up, second_grad_gate, second_grad_up,
    ) = weight_grads(
        x.reshape(tokens, -1), grads, near_hidden, full, target, own, counts,
        [first_gate.shape[1], second_gate.shape[1]],
    )
    return (
        target, first_error, second_error,
        first_grad_gate, first_grad_up, first_grad_down,
        second_grad_gate, second_grad_up, second_grad_down,
    )


def solution(mesh):
    tok = mesh.shape["tok"]
    sizes = (mesh.shape["grp"], mesh.shape["wid"])
    rows = P(("grp", "wid"), "tok")
    cols = P("tok", ("grp", "wid"))
    return jax.shard_map(
        functools.partial(body, tok, sizes),
        mesh=mesh,
        in_specs=(rows, cols, cols, rows, cols, cols, rows, cols, cols, rows),
        out_specs=(rows, rows, rows, cols, cols, rows, cols, cols, rows),
        check_vma=False,
    )
```

```python
import functools

import jax
import jax.numpy as jnp
from jax import lax
from jax.experimental import pallas as pl
from jax.experimental.pallas import tpu as pltpu
from jax.sharding import PartitionSpec as P

MESH = pl.DeviceIdType.MESH
LANES = 128
MIB = 1024 * 1024
SLOTS = 4
FORWARD_STEPS = (2, 2, 2, 2, 2, 2, 2)
BACKWARD_STEPS = (2, 2, 2, 2, 2, 2, 2)
FORWARD_GROUP = 3
BACKWARD_GROUP = 4
STEP_MIB = 50
F32 = jnp.float32
BF16 = jnp.bfloat16


def matmul(left, right):
    return jnp.dot(left, right, preferred_element_type=F32)


def outer_cols(left, right):
    return lax.dot_general(left, right, (((1,), (1,)), ((), ())), preferred_element_type=F32)


def remote(src, dst, send, recv, where):
    return pltpu.make_async_remote_copy(
        src_ref=src, dst_ref=dst, send_sem=send, recv_sem=recv,
        device_id=where, device_id_type=MESH,
    )


def relay(dims, steps, produce, finish, consume, partial, out, span, bufs, sems, prepare):
    na, nb, jobs, slots = dims
    side = nb - 1
    ay_out, ay_in, az_out, az_in, bz_out, bz_in, by_out, by_in = bufs
    (say, ray, saz, raz, sbz, rbz, sby, rby,
     tay, uay, taz, uaz, tbz, ubz, tby, uby) = sems

    me = lax.axis_index("tok")
    hi, lo = me // nb, lax.rem(me, nb)
    peers = [lax.rem(lo + d, nb) for d in range(1, nb)]
    beside = [{"tok": hi * nb + p} for p in peers]
    pos = [hi, na - 1 - hi]
    far = [na - 1 - p for p in pos]
    onward = [
        {"tok": lax.rem(hi + 1, na) * nb + lo}, {"tok": lax.rem(hi + na - 1, na) * nb + lo}
    ]
    back = onward[::-1]
    end = (hi == 0) | (hi == na - 1)
    turn = jnp.where(hi == na - 1, 0, 1)

    if prepare is not None:
        barrier = pltpu.get_barrier_semaphore()
        for where in beside:
            pl.semaphore_signal(barrier, inc=1, device_id=where, device_id_type=MESH)
        for d in range(2):
            @pl.when(pos[d] < na - 1)
            def _(d=d):
                pl.semaphore_signal(barrier, inc=1, device_id=onward[d], device_id_type=MESH)
        prepare(barrier, side + jnp.where(end, 1, 2))

    def a_block(y, d):
        return y * 2 + d

    def b_block(y, d):
        return 2 * nb + d * nb + y

    def piece(block, j, count=1):
        return out.at[pl.ds(block, count), :, pl.ds(pl.multiple_of(j * span, LANES), span)]

    def copy_ay(j, k):
        return remote(ay_out.at[j, k], ay_in.at[j, k], say.at[j, k], ray.at[j, k], beside[k])

    def copy_az(j, d):
        return remote(az_out.at[j, d], az_in.at[j, d], saz.at[j, d], raz.at[j, d], onward[d])

    def copy_bz(j, d):
        return remote(bz_out.at[j, d], bz_in.at[j, d], sbz.at[j, d], rbz.at[j, d], onward[d])

    def copy_by(j, k):
        return remote(by_out.at[j, k], by_in.at[j, k], sby.at[j, k], rby.at[j, k], beside[k])

    def spread_az(j, d):
        here = piece(a_block(lo, d), j)
        return remote(here, here, taz.at[j, d], uaz.at[j, d], back[d])

    def spread_ay(j, d, k):
        here = piece(a_block(lo, d), j)
        return remote(here, here, tay.at[j, d, k], uay.at[j, d, k], beside[k])

    def spread_by(j, k):
        here = piece(b_block(lo, turn), j)
        return remote(here, here, tby.at[j, k], uby.at[j, k], beside[k])

    def spread_bz(j, d):
        here = piece(b_block(0, d), j, nb)
        return remote(here, here, tbz.at[j, d], ubz.at[j, d], back[d])

    def on(j, condition=None):
        inside = (j >= 0) & (j < jobs)
        return pl.when(inside if condition is None else inside & condition)

    def ready(j):
        slot = lax.rem(j, slots)
        produce(j, slot)
        for k in range(side):
            ay_out[j, k] = partial[slot, pl.ds(peers[k] * 2, 2)].astype(BF16)
        for d in range(2):
            @pl.when(pos[d] == 0)
            def _(d=d):
                bz_out[j, d] = partial[slot, pl.ds(b_block(0, d), nb)].astype(BF16)

    def begin(j):
        for k in range(side):
            copy_ay(j, k).start()
        for d in range(2):
            @pl.when(pos[d] == 0)
            def _(d=d):
                copy_bz(j, d).start()

    def pair(j):
        slot = lax.rem(j, slots)
        for k in range(side):
            copy_ay(j, k).wait_recv()
        for d in range(2):
            total = partial[slot, a_block(lo, d)]
            for k in range(side):
                total = total + ay_in[j, k, d].astype(F32)
            partial[slot, a_block(lo, d)] = total

            @pl.when(pos[d] == 0)
            def _(d=d, total=total):
                az_out[j, d] = total.astype(BF16)
                copy_az(j, d).start()

    def along_a(j, d):
        slot = lax.rem(j, slots)
        copy_az(j, d).wait_recv()
        total = partial[slot, a_block(lo, d)] + az_in[j, d].astype(F32)

        @pl.when(pos[d] < na - 1)
        def _():
            az_out[j, d] = total.astype(BF16)
            copy_az(j, d).start()

        @pl.when(pos[d] == na - 1)
        def _():
            finish(j, 0, a_block(lo, d), total)
            spread_az(j, d).start()
            for k in range(side):
                spread_ay(j, d, k).start()

    def along_b(j, d):
        slot = lax.rem(j, slots)
        copy_bz(j, d).wait_recv()

        @pl.when(pos[d] < na - 1)
        def _():
            for y in range(nb):
                total = partial[slot, b_block(y, d)] + bz_in[j, d, y].astype(F32)
                bz_out[j, d, y] = total.astype(BF16)
            copy_bz(j, d).start()

        @pl.when(pos[d] == na - 1)
        def _():
            for k in range(side):
                total = partial[slot, b_block(peers[k], d)]
                total = total + bz_in[j, d, peers[k]].astype(F32)
                by_out[j, k] = total.astype(BF16)
                copy_by(j, k).start()
            total = partial[slot, b_block(lo, d)] + bz_in[j, d, lo].astype(F32)
            partial[slot, b_block(lo, d)] = total

    def corner(j):
        slot = lax.rem(j, slots)
        block = b_block(lo, turn)
        total = partial[slot, block]
        for k in range(side):
            copy_by(j, k).wait_recv()
            total = total + by_in[j, k].astype(F32)
        finish(j, 1, block, total)
        for k in range(side):
            spread_by(j, k).start()

    def leave_b(j):
        for k in range(side):
            spread_by(j, k).wait_recv()
        for d in range(2):
            @pl.when(pos[d] == na - 1)
            def _(d=d):
                spread_bz(j, d).start()

    def pass_a(j, d):
        spread_az(j, d).wait_recv()

        @pl.when(far[d] < na - 1)
        def _():
            spread_az(j, d).start()

        for k in range(side):
            spread_ay(j, d, k).start()

    def pass_b(j, d):
        spread_bz(j, d).wait_recv()

        @pl.when(far[d] < na - 1)
        def _():
            spread_bz(j, d).start()

    start_a, walk_a, walk_b, turn_b, turn_c, open_a, open_b = steps
    top = start_a + walk_a * (na - 1)
    turn_at = walk_b * (na - 1) + turn_b
    leave_at = turn_at + turn_c
    done = 1 + max(top + open_a * na, leave_at + open_b * (na - 1))

    def tick(t, carry):
        on(t)(functools.partial(begin, t))
        j = t - start_a
        on(j)(functools.partial(pair, j))
        for d in range(2):
            j = t - walk_b * pos[d]
            on(j, pos[d] > 0)(functools.partial(along_b, j, d))
        for d in range(2):
            j = t - start_a - walk_a * pos[d]
            on(j, pos[d] > 0)(functools.partial(along_a, j, d))
        j = t - turn_at
        on(j, end)(functools.partial(corner, j))
        j = t - leave_at
        on(j, end)(functools.partial(leave_b, j))
        for d in range(2):
            j = t - top - open_a * far[d]
            on(j, far[d] > 0)(functools.partial(pass_a, j, d))
        for d in range(2):
            j = t - leave_at - open_b * far[d]
            on(j, far[d] > 0)(functools.partial(pass_b, j, d))
        on(t + 1)(functools.partial(ready, t + 1))
        j = t - done
        on(j)(functools.partial(arrive, j))
        return carry

    def arrive(j):
        for k in range(side):
            for d in range(2):
                spread_ay(j, d, k).wait_recv()
        consume(j)

    ready(0)
    lax.fori_loop(0, jobs + done, tick, 0)

    def drain(j, carry):
        for k in range(side):
            copy_ay(j, k).wait_send()
            for d in range(2):
                spread_ay(j, d, k).wait_send()
        for d in range(2):
            @pl.when(pos[d] < na - 1)
            def _(d=d):
                copy_az(j, d).wait_send()
                copy_bz(j, d).wait_send()

            @pl.when(far[d] < na - 1)
            def _(d=d):
                spread_az(j, d).wait_send()
                spread_bz(j, d).wait_send()

        @pl.when(end)
        def _():
            for k in range(side):
                copy_by(j, k).wait_send()
                spread_by(j, k).wait_send()

        return carry

    return lambda: lax.fori_loop(0, jobs, drain, 0)


def relay_scratch(dims, rows, width):
    na, nb, jobs, slots = dims
    side = max(nb - 1, 1)
    dma = pltpu.SemaphoreType.DMA

    def room(*shape):
        return pltpu.VMEM((jobs,) + shape + (rows, width), BF16)

    bufs = [
        room(side, 2), room(side, 2), room(2), room(2),
        room(2, nb), room(2, nb), room(side), room(side),
    ]
    counts = [(side,), (2,), (2,), (side,), (2, side), (2,), (2,), (side,)]
    sems = [dma((jobs,) + c) for c in counts for _ in range(2)]
    partial = pltpu.VMEM((slots, 4 * nb, rows, width), F32)
    return [partial] + bufs + sems


def ring_slots(na, steps):
    return 2 + max(steps[0] + steps[1] * (na - 1), steps[2] * (na - 1) + steps[3])


def layout_of(tok, tokens):
    na = 4 if tok % 4 == 0 else tok
    nb = tok // na
    return na, nb, tokens // (4 * nb)


def plane(sizes):
    ngrp, nwid = sizes
    g, w = lax.axis_index("grp"), lax.axis_index("wid")
    spots = [
        ((d, e), lax.rem(g + d, ngrp), lax.rem(w + e, nwid))
        for d in range(ngrp) for e in range(nwid) if d or e
    ]
    return g * nwid + w, [(step, p * nwid + q, {"grp": p, "wid": q}) for step, p, q in spots]


def spreader(sizes, view, mine, sems):
    ngrp, nwid = sizes
    send, recv = sems
    g, w = lax.axis_index("grp"), lax.axis_index("wid")

    def copy(d, e, block, source=None):
        n = d * nwid + e - 1
        if e == 0:
            where = {"grp": lax.rem(g + d, ngrp)}
        else:
            where = {"wid": lax.rem(w + e, nwid)}
        here = view(block)
        return remote(here if source is None else source, here, send.at[n], recv.at[n], where)

    direct = [(d, 0) for d in range(1, ngrp)] + [(0, e) for e in range(1, nwid)]
    handed = [(d, e) for d in range(1, ngrp) for e in range(1, nwid)]

    def origin(d):
        return lax.rem(g + ngrp - d, ngrp) * nwid + w

    def first():
        for d, e in direct:
            copy(d, e, g * nwid + w, mine).start()

    def second():
        for d in range(1, ngrp):
            copy(d, 0, g * nwid + w).wait_recv()
        for d, e in handed:
            copy(d, e, origin(d)).start()

    def last():
        for e in range(1, nwid):
            copy(0, e, g * nwid + w).wait_recv()
        for d, e in handed:
            copy(d, e, origin(d)).wait_recv()

    def close():
        for d, e in direct + handed:
            copy(d, e, g * nwid + w).wait_send()

    return first, second, last, close


def step_kernel(dims, dims_back, counts, group, sizes, *refs):
    na, nb, jobs, slots = dims
    many = len(counts)
    x_ref = refs[0]
    weights = [refs[1 + 2 * i: 3 + 2 * i] for i in range(many)]
    downs = refs[1 + 2 * many: 1 + 3 * many]
    (
        x, turned, target, own, full, grads, out, kept, near,
        held, loaded, below, lowered, stored, total_of, shares, got,
        sx, rx, ss, rs, se, re,
    ) = refs[1 + 3 * many: 24 + 3 * many]
    rest = refs[24 + 3 * many:]
    partial, bufs, sems = rest[0], rest[1:9], rest[9:25]
    partial_back, bufs_back, sems_back = rest[25], rest[26:34], rest[34:]
    starts = [sum(counts[:i]) for i in range(many + 1)]
    rows = out.shape[1]
    kept_jobs = kept.shape[2] // (2 * LANES * group)
    near_units = starts[many - 1]
    near_job = (near_units - 1) // group
    members, height, features = full.shape[1:]
    pieces = ss.shape[0]
    step = features // pieces
    me, places = plane(sizes)

    def fetch(ref, column, slot, u, i):
        return pltpu.make_async_copy(
            ref.at[:, pl.ds(pl.multiple_of(column, LANES), LANES)],
            held.at[slot, u, :, pl.ds(i * LANES, LANES)],
            loaded.at[slot, u, i],
        )

    def load(j):
        slot = lax.rem(j, SLOTS)
        for u in range(group):
            c = j * group + u
            for n, pair in enumerate(weights):
                @pl.when((c >= starts[n]) & (c < starts[n + 1]))
                def _(u=u, c=c, n=n, pair=pair):
                    for i in range(2):
                        fetch(pair[i], (c - starts[n]) * LANES, slot, u, i).start()

    def below_copy(c):
        slot = lax.rem(c, below.shape[0])
        row = pl.multiple_of((c - near_units) * LANES, LANES)
        return pltpu.make_async_copy(
            downs[many - 1].at[pl.ds(row, LANES), :], below.at[slot], lowered.at[slot]
        )

    def near_copy(n):
        height_n = counts[n] * LANES
        return pltpu.make_async_copy(
            downs[n], near.at[pl.ds(starts[n] * LANES, height_n), :], stored.at[n]
        )

    xs = spreader(sizes, lambda block: x.at[block], x_ref, (sx, rx))

    def share(n, p, k, block, where):
        cols = pl.ds(p * step, step)
        return remote(
            shares.at[n, block, :, cols], got.at[k, n, :, cols],
            ss.at[p, n, k], rs.at[p, n, k], where,
        )

    def give(n):
        for p in range(pieces):
            cols = pl.ds(p * step, step)
            shares[n, :, :, cols] = total_of[n, :, cols].astype(BF16).reshape(
                members, height, step
            )
            for k, (_, block, where) in enumerate(places):
                share(n, p, k, block, where).start()

    def prepare(barrier, count):
        for _, _, where in places:
            pl.semaphore_signal(barrier, inc=1, device_id=where, device_id_type=MESH)
        for j in range(min(SLOTS, jobs)):
            load(j)
        for n in range(many - 1):
            near_copy(n).start()
        for c in range(near_units, min(near_units + below.shape[0], starts[-1])):
            below_copy(c).start()
        total_of[...] = jnp.zeros_like(total_of)
        x[me] = x_ref[...]
        pl.semaphore_wait(barrier, count + len(places))
        xs[0]()
        xs[1]()
        xs[2]()

    def produce(j, part):
        slot = lax.rem(j, SLOTS)
        left = x[...].reshape(members * height, features)
        for u in range(group):
            c = j * group + u

            @pl.when(c < starts[-1])
            def _(u=u):
                for i in range(2):
                    fetch(weights[0][0], 0, slot, u, i).wait()
                product = matmul(left, held[slot, u])
                partial[part, :, :, pl.ds(u * 2 * LANES, 2 * LANES)] = product.reshape(
                    4 * nb, rows, 2 * LANES
                )

            if starts[-1] % group:
                @pl.when(c >= starts[-1])
                def _(u=u):
                    partial[part, :, :, pl.ds(u * 2 * LANES, 2 * LANES)] = jnp.zeros(
                        (4 * nb, rows, 2 * LANES), F32
                    )

        @pl.when(j + SLOTS < jobs)
        def _():
            load(j + SLOTS)

    def finish(j, kind, block, total):
        for u in range(group):
            gate = total[:, u * 2 * LANES: u * 2 * LANES + LANES]
            up = total[:, u * 2 * LANES + LANES: (u + 1) * 2 * LANES]
            column = pl.multiple_of((j * group + u) * LANES, LANES)
            out[block, :, pl.ds(column, LANES)] = (
                gate / (1.0 + jnp.exp(-gate)) * up
            ).astype(BF16)

        @pl.when(j < kept_jobs)
        def _():
            wide = 2 * LANES * group
            kept[kind, :, pl.ds(pl.multiple_of(j * wide, LANES), wide)] = total

    def consume(j):
        for u in range(group):
            c = j * group + u
            column = pl.multiple_of(c * LANES, LANES)
            left = out[:, :, pl.ds(column, LANES)].reshape(members * height, LANES)

            @pl.when(c < near_units)
            def _(column=column, left=left):
                turned[pl.ds(column, LANES), :] = left.T

            for n in range(many - 1):
                @pl.when((c >= starts[n]) & (c < starts[n + 1]))
                def _(n=n, c=c, column=column, left=left):
                    pl.when(c == starts[n])(lambda: near_copy(n).wait())
                    total_of[n] += matmul(left, near[pl.ds(column, LANES), :])

            @pl.when((c >= near_units) & (c < starts[-1]))
            def _(c=c, left=left):
                slot = lax.rem(c, below.shape[0])
                below_copy(c).wait()
                total_of[many - 1] += matmul(left, below[slot])

                @pl.when(c + below.shape[0] < starts[-1])
                def _():
                    below_copy(c + below.shape[0]).start()

        @pl.when(j == near_job)
        def _():
            for n in range(many - 1):
                give(n)

    close = relay(
        dims, FORWARD_STEPS, produce, finish, consume, partial, out, group * LANES, bufs,
        sems, prepare,
    )

    give(many - 1)
    spreads = []
    for p in range(pieces):
        cols = pl.ds(p * step, step)
        sums = []
        for n in range(many):
            total = shares[n, me, :, cols].astype(F32)
            for k, (_, block, where) in enumerate(places):
                share(n, p, k, block, where).wait_recv()
                total = total + got[k, n, :, cols].astype(F32)
            sums.append(total)
        goal = sums[-1].astype(BF16)
        target[:, cols] = goal
        goal = goal.astype(F32)
        for n in range(many - 1):
            value = (sums[n] - goal).astype(BF16)
            own[n, :, cols] = value
            full[n, me, :, cols] = value
        spread = spreader(
            sizes, lambda block, cols=cols: full.at[:, block, :, cols], own.at[:, :, cols],
            (se.at[p], re.at[p]),
        )
        spread[0]()
        spreads.append(spread)
    for spread in spreads:
        spread[1]()
    for spread in spreads:
        spread[2]()
    close_back = backward_relay(
        dims_back, counts[:-1], full, near, kept, grads, partial_back, bufs_back, sems_back
    )
    for spread in spreads + [xs]:
        spread[3]()
    for n in range(many):
        for p in range(pieces):
            for k, (_, block, where) in enumerate(places):
                share(n, p, k, block, where).wait_send()
    close()
    close_back()


def forward(inputs, weights, downs, tok, sizes):
    height, features = inputs.shape
    members = sizes[0] * sizes[1]
    tokens = members * height
    na, nb, rows = layout_of(tok, tokens)
    weights = [padded(w) for w in weights]
    downs = [jnp.pad(d, ((0, -d.shape[0] % LANES), (0, 0))) for d in downs]
    counts = [w.shape[1] // LANES for w in weights[::2]]
    many = len(counts)
    group = FORWARD_GROUP
    jobs = -(-sum(counts) // group)
    dims = (na, nb, jobs, min(jobs, ring_slots(na, FORWARD_STEPS)))
    kept_jobs = -(-(sum(counts[:-1]) + BACKWARD_GROUP - 1) // group)
    width = 2 * LANES * group
    pieces = max(features // 256, 1)
    vmem = pl.BlockSpec(memory_space=pltpu.VMEM)
    hbm = pl.BlockSpec(memory_space=pltpu.HBM)
    dma = pltpu.SemaphoreType.DMA
    shape = jax.ShapeDtypeStruct
    lower = 2 * group
    near_units = sum(counts[:-1])
    jobs_back = -(-near_units // BACKWARD_GROUP)
    dims_back = (na, nb, jobs_back, min(jobs_back, ring_slots(na, BACKWARD_STEPS)))
    outs = pl.pallas_call(
        functools.partial(step_kernel, dims, dims_back, counts, group, sizes),
        out_shape=[
            shape((members, height, features), BF16),
            shape((near_units * LANES, tokens), BF16),
            shape((height, features), BF16),
            shape((many - 1, height, features), BF16),
            shape((many - 1, members, height, features), BF16),
            shape((4 * nb, rows, jobs_back * BACKWARD_GROUP * 2 * LANES), BF16),
        ],
        in_specs=[vmem] + [hbm] * (3 * many),
        out_specs=[vmem] * 6,
        scratch_shapes=[
            pltpu.VMEM((4 * nb, rows, jobs * group * LANES), BF16),
            pltpu.VMEM((2, rows, kept_jobs * width), F32),
            pltpu.VMEM((near_units * LANES, features), BF16),
            pltpu.VMEM((SLOTS, group, features, 2 * LANES), BF16), dma((SLOTS, group, 2)),
            pltpu.VMEM((lower, LANES, features), BF16), dma((lower,)), dma((many - 1,)),
            pltpu.VMEM((many, tokens, features), F32),
            pltpu.VMEM((many, members, height, features), BF16),
            pltpu.VMEM((members - 1, many, height, features), BF16),
            dma((members - 1,)), dma((members - 1,)),
            dma((pieces, many, members - 1)), dma((pieces, many, members - 1)),
            dma((pieces, members - 1)), dma((pieces, members - 1)),
        ] + relay_scratch(dims, rows, width)
        + relay_scratch(dims_back, rows, BACKWARD_GROUP * LANES),
        compiler_params=pltpu.CompilerParams(
            collective_id=2, has_side_effects=True, vmem_limit_bytes=STEP_MIB * MIB
        ),
        name="distill_step",
    )(inputs, *weights, *downs)
    return outs, counts


def backward_relay(dims, counts, full, near, kept, out, partial, bufs, sems):
    na, nb, jobs, slots = dims
    many = len(counts)
    group = BACKWARD_GROUP
    starts = [sum(counts[:i]) for i in range(many + 1)]
    rows = out.shape[1]
    features = full.shape[3]

    def produce(j, part):
        for u in range(group):
            c = j * group + u
            for n in range(many):
                @pl.when((c >= starts[n]) & (c < starts[n + 1]))
                def _(u=u, c=c, n=n):
                    error = full[n].reshape(4 * nb * rows, features)
                    row = pl.multiple_of(c * LANES, LANES)
                    product = outer_cols(error, near[pl.ds(row, LANES), :])
                    partial[part, :, :, pl.ds(u * LANES, LANES)] = product.reshape(
                        4 * nb, rows, LANES
                    )

            @pl.when(c >= starts[many])
            def _(u=u):
                partial[part, :, :, pl.ds(u * LANES, LANES)] = jnp.zeros(
                    (4 * nb, rows, LANES), F32
                )

    def finish(j, kind, block, total):
        for u in range(group):
            column = pl.multiple_of((j * group + u) * 2 * LANES, LANES)
            gate = kept[kind, :, pl.ds(column, LANES)]
            up = kept[kind, :, pl.ds(column + LANES, LANES)]
            value = total[:, u * LANES: (u + 1) * LANES]
            s = 1.0 / (1.0 + jnp.exp(-gate))
            out[block, :, pl.ds(column, LANES)] = (
                value * up * s * (1.0 + gate * (1.0 - s))
            ).astype(BF16)
            out[block, :, pl.ds(column + LANES, LANES)] = (value * gate * s).astype(BF16)

    return relay(
        dims, BACKWARD_STEPS, produce, finish, lambda j: None, partial, out,
        group * 2 * LANES, bufs, sems, None,
    )


def padded(x):
    return jnp.pad(x, ((0, 0), (0, -x.shape[1] % LANES)))


def outer_kernel(counts, columns, grads, turned, full, target, own, *outs):
    many = len(counts)
    tokens = columns.shape[0]
    outs[0][...] = target[...]
    for n in range(many):
        outs[1 + n][...] = own[n]
    downs = outs[1 + many: 1 + 2 * many]
    sides = outs[1 + 2 * many:]
    left = columns[...].T
    c = 0
    for n, count in enumerate(counts):
        gate, up = sides[2 * n], sides[2 * n + 1]
        error = full[n].reshape(tokens, full.shape[3])
        height = downs[n].shape[0]
        at = c * LANES
        downs[n][...] = matmul(turned[at: at + height, :], error).astype(BF16)
        for u in range(count):
            product = matmul(left, grads[:, c * 2 * LANES: (c + 1) * 2 * LANES]).astype(BF16)
            size = min(LANES, gate.shape[1] - u * LANES)
            gate[:, u * LANES: u * LANES + size] = product[:, :size]
            up[:, u * LANES: u * LANES + size] = product[:, LANES: LANES + size]
            c += 1


def weight_grads(columns, grads, turned, full, target, own, counts, widths):
    tokens, features = columns.shape
    tile = 2 * LANES if features % (2 * LANES) == 0 else features
    many, members, height = full.shape[:3]
    out_bytes = 6 * features * sum(widths)
    sides = [w for w in widths for _ in range(2)]
    shape = jax.ShapeDtypeStruct
    whole = pl.BlockSpec(memory_space=pltpu.VMEM)
    lane = pl.BlockSpec((height, tile), lambda i: (0, i))
    return pl.pallas_call(
        functools.partial(outer_kernel, counts),
        grid=(features // tile,),
        out_shape=[shape((height, features), BF16)] * (1 + many)
        + [shape((w, features), BF16) for w in widths]
        + [shape((features, w), BF16) for w in sides],
        in_specs=[
            pl.BlockSpec((tokens, tile), lambda i: (0, i)), whole, whole,
            pl.BlockSpec((many, members, height, tile), lambda i: (0, 0, 0, i)),
            lane, pl.BlockSpec((many, height, tile), lambda i: (0, 0, i)),
        ],
        out_specs=[lane] * (1 + many)
        + [pl.BlockSpec((w, tile), lambda i: (0, i)) for w in widths]
        + [pl.BlockSpec((tile, w), lambda i: (i, 0)) for w in sides],
        compiler_params=pltpu.CompilerParams(vmem_limit_bytes=40 * MIB),
        cost_estimate=pl.CostEstimate(
            flops=tokens * out_bytes, bytes_accessed=out_bytes, transcendentals=0
        ),
        name="weight_grads",
    )(columns, grads, turned, full, target, own)


def body(
    tok, sizes, inputs, parent_gate, parent_up, parent_down, first_gate, first_up, first_down,
    second_gate, second_up, second_down,
):
    weights = (first_gate, first_up, second_gate, second_up, parent_gate, parent_up)
    downs = (first_down, second_down, parent_down)
    (x, turned, target, own, full, grads), counts = forward(
        inputs, weights, downs, tok, sizes
    )
    tokens = x.shape[0] * x.shape[1]
    counts = counts[:-1]
    (
        target, first_error, second_error, first_grad_down, second_grad_down,
        first_grad_gate, first_grad_up, second_grad_gate, second_grad_up,
    ) = weight_grads(
        x.reshape(tokens, -1), grads.reshape(tokens, -1), turned, full, target, own, counts,
        [first_gate.shape[1], second_gate.shape[1]],
    )
    return (
        target, first_error, second_error,
        first_grad_gate, first_grad_up, first_grad_down,
        second_grad_gate, second_grad_up, second_grad_down,
    )


def solution(mesh):
    tok = mesh.shape["tok"]
    sizes = (mesh.shape["grp"], mesh.shape["wid"])
    rows = P(("grp", "wid"), "tok")
    cols = P("tok", ("grp", "wid"))
    return jax.shard_map(
        functools.partial(body, tok, sizes),
        mesh=mesh,
        in_specs=(rows, cols, cols, rows, cols, cols, rows, cols, cols, rows),
        out_specs=(rows, rows, rows, cols, cols, rows, cols, cols, rows),
        check_vma=False,
    )
```

```python
import functools

import jax
import jax.numpy as jnp
from jax import lax
from jax.experimental import pallas as pl
from jax.experimental.pallas import tpu as pltpu
from jax.sharding import PartitionSpec as P

MESH = pl.DeviceIdType.MESH
LANES = 128
MIB = 1024 * 1024
SLOTS = 4
FORWARD_STEPS = (3, 3, 3, 3, 3, 3, 3)
BACKWARD_STEPS = (2, 2, 2, 2, 2, 2, 2)
FORWARD_GROUP = 3
BACKWARD_GROUP = 5
STEP_MIB = 50
F32 = jnp.float32
BF16 = jnp.bfloat16


def matmul(left, right):
    return jnp.dot(left, right, preferred_element_type=F32)


def outer_cols(left, right):
    return lax.dot_general(left, right, (((1,), (1,)), ((), ())), preferred_element_type=F32)


def remote(src, dst, send, recv, where):
    return pltpu.make_async_remote_copy(
        src_ref=src, dst_ref=dst, send_sem=send, recv_sem=recv,
        device_id=where, device_id_type=MESH,
    )


def relay(dims, steps, produce, finish, consume, partial, out, span, bufs, sems, prepare):
    na, nb, jobs, slots = dims
    side = nb - 1
    ay_out, ay_in, az_out, az_in, bz_out, bz_in, by_out, by_in = bufs
    (say, ray, saz, raz, sbz, rbz, sby, rby,
     tay, uay, taz, uaz, tbz, ubz, tby, uby) = sems

    me = lax.axis_index("tok")
    hi, lo = me // nb, lax.rem(me, nb)
    peers = [lax.rem(lo + d, nb) for d in range(1, nb)]
    beside = [{"tok": hi * nb + p} for p in peers]
    pos = [hi, na - 1 - hi]
    far = [na - 1 - p for p in pos]
    onward = [
        {"tok": lax.rem(hi + 1, na) * nb + lo}, {"tok": lax.rem(hi + na - 1, na) * nb + lo}
    ]
    back = onward[::-1]
    end = (hi == 0) | (hi == na - 1)
    turn = jnp.where(hi == na - 1, 0, 1)

    if prepare is not None:
        barrier = pltpu.get_barrier_semaphore()
        for where in beside:
            pl.semaphore_signal(barrier, inc=1, device_id=where, device_id_type=MESH)
        for d in range(2):
            @pl.when(pos[d] < na - 1)
            def _(d=d):
                pl.semaphore_signal(barrier, inc=1, device_id=onward[d], device_id_type=MESH)
        prepare(barrier, side + jnp.where(end, 1, 2))

    def a_block(y, d):
        return y * 2 + d

    def b_block(y, d):
        return 2 * nb + d * nb + y

    def piece(block, j, count=1):
        return out.at[pl.ds(block, count), :, pl.ds(pl.multiple_of(j * span, LANES), span)]

    def copy_ay(j, k):
        return remote(ay_out.at[j, k], ay_in.at[j, k], say.at[k], ray.at[j, k], beside[k])

    def copy_az(j, d):
        return remote(az_out.at[j, d], az_in.at[j, d], saz.at[d], raz.at[j, d], onward[d])

    def copy_bz(j, d):
        return remote(bz_out.at[j, d], bz_in.at[j, d], sbz.at[d], rbz.at[j, d], onward[d])

    def copy_by(j, k):
        return remote(by_out.at[j, k], by_in.at[j, k], sby.at[k], rby.at[j, k], beside[k])

    def spread_az(j, d):
        here = piece(a_block(lo, d), j)
        return remote(here, here, taz.at[d], uaz.at[j, d], back[d])

    def spread_ay(j, d, k):
        here = piece(a_block(lo, d), j)
        return remote(here, here, tay.at[d, k], uay.at[j, d, k], beside[k])

    def spread_by(j, k):
        here = piece(b_block(lo, turn), j)
        return remote(here, here, tby.at[k], uby.at[j, k], beside[k])

    def spread_bz(j, d):
        here = piece(b_block(0, d), j, nb)
        return remote(here, here, tbz.at[d], ubz.at[j, d], back[d])

    def on(j, condition=None):
        inside = (j >= 0) & (j < jobs)
        return pl.when(inside if condition is None else inside & condition)

    def ready(j):
        slot = lax.rem(j, slots)
        produce(j, slot)
        for k in range(side):
            ay_out[j, k] = partial[slot, pl.ds(peers[k] * 2, 2)].astype(BF16)
        for d in range(2):
            @pl.when(pos[d] == 0)
            def _(d=d):
                bz_out[j, d] = partial[slot, pl.ds(b_block(0, d), nb)].astype(BF16)

    def begin(j):
        for k in range(side):
            copy_ay(j, k).start()
        for d in range(2):
            @pl.when(pos[d] == 0)
            def _(d=d):
                copy_bz(j, d).start()

    def pair(j):
        slot = lax.rem(j, slots)
        for k in range(side):
            copy_ay(j, k).wait_recv()
        for d in range(2):
            total = partial[slot, a_block(lo, d)]
            for k in range(side):
                total = total + ay_in[j, k, d].astype(F32)
            partial[slot, a_block(lo, d)] = total

            @pl.when(pos[d] == 0)
            def _(d=d, total=total):
                az_out[j, d] = total.astype(BF16)
                copy_az(j, d).start()

    def along_a(j, d):
        slot = lax.rem(j, slots)
        copy_az(j, d).wait_recv()
        total = partial[slot, a_block(lo, d)] + az_in[j, d].astype(F32)

        @pl.when(pos[d] < na - 1)
        def _():
            az_out[j, d] = total.astype(BF16)
            copy_az(j, d).start()

        @pl.when(pos[d] == na - 1)
        def _():
            finish(j, 0, a_block(lo, d), total)
            spread_az(j, d).start()
            for k in range(side):
                spread_ay(j, d, k).start()

    def along_b(j, d):
        slot = lax.rem(j, slots)
        copy_bz(j, d).wait_recv()

        @pl.when(pos[d] < na - 1)
        def _():
            for y in range(nb):
                total = partial[slot, b_block(y, d)] + bz_in[j, d, y].astype(F32)
                bz_out[j, d, y] = total.astype(BF16)
            copy_bz(j, d).start()

        @pl.when(pos[d] == na - 1)
        def _():
            for k in range(side):
                total = partial[slot, b_block(peers[k], d)]
                total = total + bz_in[j, d, peers[k]].astype(F32)
                by_out[j, k] = total.astype(BF16)
                copy_by(j, k).start()
            total = partial[slot, b_block(lo, d)] + bz_in[j, d, lo].astype(F32)
            partial[slot, b_block(lo, d)] = total

    def corner(j):
        slot = lax.rem(j, slots)
        block = b_block(lo, turn)
        total = partial[slot, block]
        for k in range(side):
            copy_by(j, k).wait_recv()
            total = total + by_in[j, k].astype(F32)
        finish(j, 1, block, total)
        for k in range(side):
            spread_by(j, k).start()

    def leave_b(j):
        for k in range(side):
            spread_by(j, k).wait_recv()
        for d in range(2):
            @pl.when(pos[d] == na - 1)
            def _(d=d):
                spread_bz(j, d).start()

    def pass_a(j, d):
        spread_az(j, d).wait_recv()

        @pl.when(far[d] < na - 1)
        def _():
            spread_az(j, d).start()

        for k in range(side):
            spread_ay(j, d, k).start()

    def pass_b(j, d):
        spread_bz(j, d).wait_recv()

        @pl.when(far[d] < na - 1)
        def _():
            spread_bz(j, d).start()

    start_a, walk_a, walk_b, turn_b, turn_c, open_a, open_b = steps
    top = start_a + walk_a * (na - 1)
    turn_at = walk_b * (na - 1) + turn_b
    leave_at = turn_at + turn_c
    done = 1 + max(top + open_a * na, leave_at + open_b * (na - 1))

    def tick(t, carry):
        on(t)(functools.partial(begin, t))
        j = t - start_a
        on(j)(functools.partial(pair, j))
        for d in range(2):
            j = t - walk_b * pos[d]
            on(j, pos[d] > 0)(functools.partial(along_b, j, d))
        for d in range(2):
            j = t - start_a - walk_a * pos[d]
            on(j, pos[d] > 0)(functools.partial(along_a, j, d))
        j = t - turn_at
        on(j, end)(functools.partial(corner, j))
        j = t - leave_at
        on(j, end)(functools.partial(leave_b, j))
        for d in range(2):
            j = t - top - open_a * far[d]
            on(j, far[d] > 0)(functools.partial(pass_a, j, d))
        for d in range(2):
            j = t - leave_at - open_b * far[d]
            on(j, far[d] > 0)(functools.partial(pass_b, j, d))
        on(t + 1)(functools.partial(ready, t + 1))
        j = t - done
        on(j)(functools.partial(arrive, j))
        return carry

    def arrive(j):
        for k in range(side):
            for d in range(2):
                spread_ay(j, d, k).wait_recv()
        consume(j)

    ready(0)
    lax.fori_loop(0, jobs + done, tick, 0)

    def drain():
        def spent(block, count, send, recv, where):
            here = out.at[pl.ds(block, count)]
            remote(here, here, send, recv, where).wait_send()

        for k in range(side):
            remote(
                ay_out.at[:, k], ay_in.at[:, k], say.at[k], ray.at[0, k], beside[k]
            ).wait_send()
            for d in range(2):
                spent(a_block(lo, d), 1, tay.at[d, k], uay.at[0, d, k], beside[k])
        for d in range(2):
            @pl.when(pos[d] < na - 1)
            def _(d=d):
                remote(
                    az_out.at[:, d], az_in.at[:, d], saz.at[d], raz.at[0, d], onward[d]
                ).wait_send()
                remote(
                    bz_out.at[:, d], bz_in.at[:, d], sbz.at[d], rbz.at[0, d], onward[d]
                ).wait_send()

            @pl.when(far[d] < na - 1)
            def _(d=d):
                spent(a_block(lo, d), 1, taz.at[d], uaz.at[0, d], back[d])
                spent(b_block(0, d), nb, tbz.at[d], ubz.at[0, d], back[d])

        @pl.when(end)
        def _():
            for k in range(side):
                remote(
                    by_out.at[:, k], by_in.at[:, k], sby.at[k], rby.at[0, k], beside[k]
                ).wait_send()
                spent(b_block(lo, turn), 1, tby.at[k], uby.at[0, k], beside[k])

    return drain


def relay_scratch(dims, rows, width):
    na, nb, jobs, slots = dims
    side = max(nb - 1, 1)
    dma = pltpu.SemaphoreType.DMA

    def room(*shape):
        return pltpu.VMEM((jobs,) + shape + (rows, width), BF16)

    bufs = [
        room(side, 2), room(side, 2), room(2), room(2),
        room(2, nb), room(2, nb), room(side), room(side),
    ]
    counts = [(side,), (2,), (2,), (side,), (2, side), (2,), (2,), (side,)]
    sems = [dma(lead + c) for c in counts for lead in ((), (jobs,))]
    partial = pltpu.VMEM((slots, 4 * nb, rows, width), F32)
    return [partial] + bufs + sems


def ring_slots(na, steps):
    return 2 + max(steps[0] + steps[1] * (na - 1), steps[2] * (na - 1) + steps[3])


def layout_of(tok, tokens):
    na = 4 if tok % 4 == 0 else tok
    nb = tok // na
    return na, nb, tokens // (4 * nb)


def plane(sizes):
    ngrp, nwid = sizes
    g, w = lax.axis_index("grp"), lax.axis_index("wid")
    spots = [
        ((d, e), lax.rem(g + d, ngrp), lax.rem(w + e, nwid))
        for d in range(ngrp) for e in range(nwid) if d or e
    ]
    return g * nwid + w, [(step, p * nwid + q, {"grp": p, "wid": q}) for step, p, q in spots]


def spreader(sizes, view, mine, sems):
    ngrp, nwid = sizes
    send, recv = sems
    g, w = lax.axis_index("grp"), lax.axis_index("wid")

    def copy(d, e, block, source=None):
        n = d * nwid + e - 1
        if e == 0:
            where = {"grp": lax.rem(g + d, ngrp)}
        else:
            where = {"wid": lax.rem(w + e, nwid)}
        here = view(block)
        return remote(here if source is None else source, here, send.at[n], recv.at[n], where)

    direct = [(d, 0) for d in range(1, ngrp)] + [(0, e) for e in range(1, nwid)]
    handed = [(d, e) for d in range(1, ngrp) for e in range(1, nwid)]

    def origin(d):
        return lax.rem(g + ngrp - d, ngrp) * nwid + w

    def first():
        for d, e in direct:
            copy(d, e, g * nwid + w, mine).start()

    def second():
        for d in range(1, ngrp):
            copy(d, 0, g * nwid + w).wait_recv()
        for d, e in handed:
            copy(d, e, origin(d)).start()

    def last():
        for e in range(1, nwid):
            copy(0, e, g * nwid + w).wait_recv()
        for d, e in handed:
            copy(d, e, origin(d)).wait_recv()

    def close():
        for d, e in direct + handed:
            copy(d, e, g * nwid + w).wait_send()

    return first, second, last, close


def step_kernel(dims, dims_back, counts, group, sizes, *refs):
    na, nb, jobs, slots = dims
    many = len(counts)
    x_ref = refs[0]
    weights = [refs[1 + 2 * i: 3 + 2 * i] for i in range(many)]
    downs = refs[1 + 2 * many: 1 + 3 * many]
    (
        x, turned, target, own, full, grads, out, kept, near,
        held, loaded, below, lowered, stored, total_of, shares, got,
        sx, rx, ss, rs, se, re,
    ) = refs[1 + 3 * many: 24 + 3 * many]
    rest = refs[24 + 3 * many:]
    partial, bufs, sems = rest[0], rest[1:9], rest[9:25]
    partial_back, bufs_back, sems_back = rest[25], rest[26:34], rest[34:]
    starts = [sum(counts[:i]) for i in range(many + 1)]
    rows = out.shape[1]
    kept_jobs = kept.shape[2] // (2 * LANES * group)
    near_units = starts[many - 1]
    near_job = (near_units - 1) // group
    members, height, features = full.shape[1:]
    pieces = rs.shape[0]
    step = features // pieces
    me, places = plane(sizes)

    cases = cases_of(starts, group, jobs)
    first_below = near_units // group
    depth = below.shape[0]
    side_width = group * LANES

    def between(j, low, high):
        return pl.when((j >= low) & (j < high))

    def window(at, size):
        return pl.ds(pl.multiple_of(at * LANES, LANES), size * LANES)

    def load(j):
        slot = lax.rem(j, SLOTS)
        for low, high, spans in cases:
            @between(j, low, high)
            def _(spans=spans):
                for n, u, v in spans:
                    for i in range(2):
                        pltpu.make_async_copy(
                            weights[n][i].at[:, window(j * group + u - starts[n], v - u)],
                            held.at[slot, :, pl.ds(i * side_width + u * LANES, (v - u) * LANES)],
                            loaded.at[slot],
                        ).start()

    def below_copy(j, u, v):
        slot = lax.rem(j, depth)
        return pltpu.make_async_copy(
            downs[many - 1].at[window(j * group + u - near_units, v - u), :],
            below.at[slot, pl.ds(u * LANES, (v - u) * LANES), :], lowered.at[slot],
        )

    def load_below(j):
        for low, high, spans in cases:
            for n, u, v in spans:
                if n == many - 1:
                    @between(j, low, high)
                    def _(u=u, v=v):
                        below_copy(j, u, v).start()

    def near_copy(n):
        height_n = counts[n] * LANES
        return pltpu.make_async_copy(
            downs[n], near.at[pl.ds(starts[n] * LANES, height_n), :], stored.at[n]
        )

    xs = spreader(sizes, lambda block: x.at[block], x_ref, (sx, rx))

    def share(n, p, k, block, where):
        cols = pl.ds(p * step, step)
        return remote(
            shares.at[n, block, :, cols], got.at[k, n, :, cols],
            ss.at[n, k], rs.at[p, n, k], where,
        )

    def give(n):
        for p in range(pieces):
            cols = pl.ds(p * step, step)
            shares[n, :, :, cols] = total_of[n, :, cols].astype(BF16).reshape(
                members, height, step
            )
            for k, (_, block, where) in enumerate(places):
                share(n, p, k, block, where).start()

    def prepare(barrier, count):
        for _, _, where in places:
            pl.semaphore_signal(barrier, inc=1, device_id=where, device_id_type=MESH)
        for j in range(min(SLOTS, jobs)):
            load(j)
        for n in range(many - 1):
            near_copy(n).start()
        for j in range(first_below, min(first_below + depth, jobs)):
            load_below(j)
        total_of[...] = jnp.zeros_like(total_of)
        x[me] = x_ref[...]
        pl.semaphore_wait(barrier, count + len(places))
        xs[0]()
        xs[1]()
        xs[2]()

    def produce(j, part):
        slot = lax.rem(j, SLOTS)
        left = x[...].reshape(members * height, features)
        pltpu.make_async_copy(held.at[slot], held.at[slot], loaded.at[slot]).wait()
        partial[part] = matmul(left, held[slot]).reshape(4 * nb, rows, 2 * side_width)

        @pl.when(j + SLOTS < jobs)
        def _():
            load(j + SLOTS)

    def finish(j, kind, block, total):
        gate, up = total[:, :side_width], total[:, side_width:]
        out[block, :, window(j * group, group)] = (
            gate / (1.0 + jnp.exp(-gate)) * up
        ).astype(BF16)

        @pl.when(j < kept_jobs)
        def _():
            wide = 2 * LANES * group
            kept[kind, :, pl.ds(pl.multiple_of(j * wide, LANES), wide)] = total

    def consume(j):
        for n in range(many - 1):
            pl.when(j == starts[n] // group)(lambda n=n: near_copy(n).wait())
        for low, high, spans in cases:
            @between(j, low, high)
            def _(spans=spans):
                for n, u, v in spans:
                    here = window(j * group + u, v - u)
                    left = out[:, :, here].reshape(members * height, (v - u) * LANES)
                    if n < many - 1:
                        turned[here, :] = left.T
                        right = near[here, :]
                    else:
                        below_copy(j, u, v).wait()
                        right = below[lax.rem(j, depth), pl.ds(u * LANES, (v - u) * LANES), :]
                    total_of[n] += matmul(left, right)

        @pl.when((j >= first_below) & (j + depth < jobs))
        def _():
            load_below(j + depth)

        @pl.when(j == near_job)
        def _():
            for n in range(many - 1):
                give(n)

    close = relay(
        dims, FORWARD_STEPS, produce, finish, consume, partial, out, group * LANES, bufs,
        sems, prepare,
    )

    give(many - 1)
    spreads = []
    for p in range(pieces):
        cols = pl.ds(p * step, step)
        sums = []
        for n in range(many):
            total = shares[n, me, :, cols].astype(F32)
            for k, (_, block, where) in enumerate(places):
                share(n, p, k, block, where).wait_recv()
                total = total + got[k, n, :, cols].astype(F32)
            sums.append(total)
        goal = sums[-1].astype(BF16)
        target[:, cols] = goal
        goal = goal.astype(F32)
        for n in range(many - 1):
            value = (sums[n] - goal).astype(BF16)
            own[n, :, cols] = value
            full[n, me, :, cols] = value
        spread = spreader(
            sizes, lambda block, cols=cols: full.at[:, block, :, cols], own.at[:, :, cols],
            (se.at[p], re.at[p]),
        )
        spread[0]()
        spreads.append(spread)
    for spread in spreads:
        spread[1]()
    for spread in spreads:
        spread[2]()
    close_back = backward_relay(
        dims_back, counts[:-1], group, full, near, kept, grads, partial_back, bufs_back,
        sems_back,
    )
    for spread in spreads + [xs]:
        spread[3]()
    for n in range(many):
        for k, (_, block, where) in enumerate(places):
            remote(
                shares.at[n, block], got.at[k, n], ss.at[n, k], rs.at[0, n, k], where
            ).wait_send()
    close()
    close_back()


def forward(inputs, weights, downs, tok, sizes):
    height, features = inputs.shape
    members = sizes[0] * sizes[1]
    tokens = members * height
    na, nb, rows = layout_of(tok, tokens)
    weights = [padded(w) for w in weights]
    downs = [jnp.pad(d, ((0, -d.shape[0] % LANES), (0, 0))) for d in downs]
    counts = [w.shape[1] // LANES for w in weights[::2]]
    many = len(counts)
    group = FORWARD_GROUP if sum(counts) % FORWARD_GROUP == 0 else 1
    jobs = sum(counts) // group
    dims = (na, nb, jobs, min(jobs, ring_slots(na, FORWARD_STEPS)))
    kept_jobs = -(-(sum(counts[:-1]) + BACKWARD_GROUP - 1) // group)
    width = 2 * LANES * group
    pieces = max(features // 256, 1)
    vmem = pl.BlockSpec(memory_space=pltpu.VMEM)
    hbm = pl.BlockSpec(memory_space=pltpu.HBM)
    dma = pltpu.SemaphoreType.DMA
    shape = jax.ShapeDtypeStruct
    lower = 3
    near_units = sum(counts[:-1])
    jobs_back = -(-near_units // BACKWARD_GROUP)
    dims_back = (na, nb, jobs_back, min(jobs_back, ring_slots(na, BACKWARD_STEPS)))
    outs = pl.pallas_call(
        functools.partial(step_kernel, dims, dims_back, counts, group, sizes),
        out_shape=[
            shape((members, height, features), BF16),
            shape((near_units * LANES, tokens), BF16),
            shape((height, features), BF16),
            shape((many - 1, height, features), BF16),
            shape((many - 1, members, height, features), BF16),
            shape((4 * nb, rows, jobs_back * BACKWARD_GROUP * 2 * LANES), BF16),
        ],
        in_specs=[vmem] + [hbm] * (3 * many),
        out_specs=[vmem] * 6,
        scratch_shapes=[
            pltpu.VMEM((4 * nb, rows, jobs * group * LANES), BF16),
            pltpu.VMEM((2, rows, kept_jobs * width), F32),
            pltpu.VMEM((near_units * LANES, features), BF16),
            pltpu.VMEM((SLOTS, features, width), BF16), dma((SLOTS,)),
            pltpu.VMEM((lower, group * LANES, features), BF16), dma((lower,)), dma((many - 1,)),
            pltpu.VMEM((many, tokens, features), F32),
            pltpu.VMEM((many, members, height, features), BF16),
            pltpu.VMEM((members - 1, many, height, features), BF16),
            dma((members - 1,)), dma((members - 1,)),
            dma((many, members - 1)), dma((pieces, many, members - 1)),
            dma((pieces, members - 1)), dma((pieces, members - 1)),
        ] + relay_scratch(dims, rows, width)
        + relay_scratch(dims_back, rows, BACKWARD_GROUP * LANES),
        compiler_params=pltpu.CompilerParams(
            collective_id=2, has_side_effects=True, vmem_limit_bytes=STEP_MIB * MIB
        ),
        name="distill_step",
    )(inputs, *weights, *downs)
    return outs, counts


def backward_relay(dims, counts, kept_group, full, near, kept, out, partial, bufs, sems):
    na, nb, jobs, slots = dims
    many = len(counts)
    group = BACKWARD_GROUP
    starts = [sum(counts[:i]) for i in range(many + 1)]
    rows = out.shape[1]
    features = full.shape[3]

    cases = cases_of(starts, group, jobs)

    def produce(j, part):
        for low, high, spans in cases:
            @pl.when((j >= low) & (j < high))
            def _(spans=spans):
                for n, u, v in spans:
                    error = full[n].reshape(4 * nb * rows, features)
                    row = pl.multiple_of((j * group + u) * LANES, LANES)
                    product = outer_cols(error, near[pl.ds(row, (v - u) * LANES), :])
                    partial[part, :, :, u * LANES: v * LANES] = product.reshape(
                        4 * nb, rows, (v - u) * LANES
                    )
                last = spans[-1][2]
                if last < group:
                    partial[part, :, :, last * LANES:] = jnp.zeros(
                        (4 * nb, rows, (group - last) * LANES), F32
                    )

    def finish(j, kind, block, total):
        for u in range(group):
            column = pl.multiple_of((j * group + u) * 2 * LANES, LANES)
            c = j * group + u
            where = c // kept_group * 2 * kept_group + lax.rem(c, kept_group)
            where = pl.multiple_of(where * LANES, LANES)
            gate = kept[kind, :, pl.ds(where, LANES)]
            up = kept[kind, :, pl.ds(where + kept_group * LANES, LANES)]
            value = total[:, u * LANES: (u + 1) * LANES]
            s = 1.0 / (1.0 + jnp.exp(-gate))
            out[block, :, pl.ds(column, LANES)] = (
                value * up * s * (1.0 + gate * (1.0 - s))
            ).astype(BF16)
            out[block, :, pl.ds(column + LANES, LANES)] = (value * gate * s).astype(BF16)

    return relay(
        dims, BACKWARD_STEPS, produce, finish, lambda j: None, partial, out,
        group * 2 * LANES, bufs, sems, None,
    )


def cases_of(starts, group, jobs):
    cases = []
    for j in range(jobs):
        spans = []
        for n in range(len(starts) - 1):
            low, high = max(starts[n], j * group), min(starts[n + 1], (j + 1) * group)
            if low < high:
                spans.append((n, low - j * group, high - j * group))
        if cases and cases[-1][2] == spans:
            cases[-1] = (cases[-1][0], j + 1, spans)
        else:
            cases.append((j, j + 1, spans))
    return cases


def padded(x):
    return jnp.pad(x, ((0, 0), (0, -x.shape[1] % LANES)))


def outer_kernel(counts, columns, grads, turned, full, target, own, *outs):
    many = len(counts)
    tokens = columns.shape[0]
    outs[0][...] = target[...]
    for n in range(many):
        outs[1 + n][...] = own[n]
    downs = outs[1 + many: 1 + 2 * many]
    sides = outs[1 + 2 * many:]
    left = columns[...].T
    c = 0
    for n, count in enumerate(counts):
        gate, up = sides[2 * n], sides[2 * n + 1]
        error = full[n].reshape(tokens, full.shape[3])
        height = downs[n].shape[0]
        at = c * LANES
        downs[n][...] = matmul(turned[at: at + height, :], error).astype(BF16)
        for u in range(count):
            product = matmul(left, grads[:, c * 2 * LANES: (c + 1) * 2 * LANES]).astype(BF16)
            size = min(LANES, gate.shape[1] - u * LANES)
            gate[:, u * LANES: u * LANES + size] = product[:, :size]
            up[:, u * LANES: u * LANES + size] = product[:, LANES: LANES + size]
            c += 1


def weight_grads(columns, grads, turned, full, target, own, counts, widths):
    tokens, features = columns.shape
    tile = 2 * LANES if features % (2 * LANES) == 0 else features
    many, members, height = full.shape[:3]
    out_bytes = 6 * features * sum(widths)
    sides = [w for w in widths for _ in range(2)]
    shape = jax.ShapeDtypeStruct
    whole = pl.BlockSpec(memory_space=pltpu.VMEM)
    lane = pl.BlockSpec((height, tile), lambda i: (0, i))
    return pl.pallas_call(
        functools.partial(outer_kernel, counts),
        grid=(features // tile,),
        out_shape=[shape((height, features), BF16)] * (1 + many)
        + [shape((w, features), BF16) for w in widths]
        + [shape((features, w), BF16) for w in sides],
        in_specs=[
            pl.BlockSpec((tokens, tile), lambda i: (0, i)), whole, whole,
            pl.BlockSpec((many, members, height, tile), lambda i: (0, 0, 0, i)),
            lane, pl.BlockSpec((many, height, tile), lambda i: (0, 0, i)),
        ],
        out_specs=[lane] * (1 + many)
        + [pl.BlockSpec((w, tile), lambda i: (0, i)) for w in widths]
        + [pl.BlockSpec((tile, w), lambda i: (i, 0)) for w in sides],
        compiler_params=pltpu.CompilerParams(vmem_limit_bytes=40 * MIB),
        cost_estimate=pl.CostEstimate(
            flops=tokens * out_bytes, bytes_accessed=out_bytes, transcendentals=0
        ),
        name="weight_grads",
    )(columns, grads, turned, full, target, own)


def body(
    tok, sizes, inputs, parent_gate, parent_up, parent_down, first_gate, first_up, first_down,
    second_gate, second_up, second_down,
):
    weights = (first_gate, first_up, second_gate, second_up, parent_gate, parent_up)
    downs = (first_down, second_down, parent_down)
    (x, turned, target, own, full, grads), counts = forward(
        inputs, weights, downs, tok, sizes
    )
    tokens = x.shape[0] * x.shape[1]
    counts = counts[:-1]
    (
        target, first_error, second_error, first_grad_down, second_grad_down,
        first_grad_gate, first_grad_up, second_grad_gate, second_grad_up,
    ) = weight_grads(
        x.reshape(tokens, -1), grads.reshape(tokens, -1), turned, full, target, own, counts,
        [first_gate.shape[1], second_gate.shape[1]],
    )
    return (
        target, first_error, second_error,
        first_grad_gate, first_grad_up, first_grad_down,
        second_grad_gate, second_grad_up, second_grad_down,
    )


def solution(mesh):
    tok = mesh.shape["tok"]
    sizes = (mesh.shape["grp"], mesh.shape["wid"])
    rows = P(("grp", "wid"), "tok")
    cols = P("tok", ("grp", "wid"))
    return jax.shard_map(
        functools.partial(body, tok, sizes),
        mesh=mesh,
        in_specs=(rows, cols, cols, rows, cols, cols, rows, cols, cols, rows),
        out_specs=(rows, rows, rows, cols, cols, rows, cols, cols, rows),
        check_vma=False,
    )
```

```python
import functools

import jax
import jax.numpy as jnp
from jax import lax
from jax.experimental import pallas as pl
from jax.experimental.pallas import tpu as pltpu
from jax.sharding import PartitionSpec as P

MESH = pl.DeviceIdType.MESH
LANES = 128
MIB = 1024 * 1024
SLOTS = 4
FORWARD_STEPS = (3, 3, 3, 3, 3, 3, 3)
BACKWARD_STEPS = (2, 2, 2, 2, 2, 2, 2)
FORWARD_GROUP = 3
BACKWARD_GROUP = 5
STEP_MIB = 50
GRAD_TILE = 256
F32 = jnp.float32
BF16 = jnp.bfloat16


def matmul(left, right):
    return jnp.dot(left, right, preferred_element_type=F32)


def outer_cols(left, right):
    return lax.dot_general(left, right, (((1,), (1,)), ((), ())), preferred_element_type=F32)


def remote(src, dst, send, recv, where):
    return pltpu.make_async_remote_copy(
        src_ref=src, dst_ref=dst, send_sem=send, recv_sem=recv,
        device_id=where, device_id_type=MESH,
    )


def relay(dims, steps, produce, finish, consume, partial, out, span, bufs, sems, prepare):
    na, nb, jobs, slots = dims
    side = nb - 1
    ay_out, ay_in, az_out, az_in, bz_out, bz_in, by_out, by_in = bufs
    (say, ray, saz, raz, sbz, rbz, sby, rby,
     tay, uay, taz, uaz, tbz, ubz, tby, uby) = sems

    me = lax.axis_index("tok")
    hi, lo = me // nb, lax.rem(me, nb)
    peers = [lax.rem(lo + d, nb) for d in range(1, nb)]
    beside = [{"tok": hi * nb + p} for p in peers]
    pos = [hi, na - 1 - hi]
    far = [na - 1 - p for p in pos]
    onward = [
        {"tok": lax.rem(hi + 1, na) * nb + lo}, {"tok": lax.rem(hi + na - 1, na) * nb + lo}
    ]
    back = onward[::-1]
    end = (hi == 0) | (hi == na - 1)
    turn = jnp.where(hi == na - 1, 0, 1)

    if prepare is not None:
        barrier = pltpu.get_barrier_semaphore()
        for where in beside:
            pl.semaphore_signal(barrier, inc=1, device_id=where, device_id_type=MESH)
        for d in range(2):
            @pl.when(pos[d] < na - 1)
            def _(d=d):
                pl.semaphore_signal(barrier, inc=1, device_id=onward[d], device_id_type=MESH)
        prepare(barrier, side + jnp.where(end, 1, 2))

    def a_block(y, d):
        return y * 2 + d

    def b_block(y, d):
        return 2 * nb + d * nb + y

    def piece(block, j, count=1):
        return out.at[pl.ds(block, count), :, pl.ds(pl.multiple_of(j * span, LANES), span)]

    def copy_ay(j, k):
        return remote(ay_out.at[j, k], ay_in.at[j, k], say.at[k], ray.at[j, k], beside[k])

    def copy_az(j, d):
        return remote(az_out.at[j, d], az_in.at[j, d], saz.at[d], raz.at[j, d], onward[d])

    def copy_bz(j, d):
        return remote(bz_out.at[j, d], bz_in.at[j, d], sbz.at[d], rbz.at[j, d], onward[d])

    def copy_by(j, k):
        return remote(by_out.at[j, k], by_in.at[j, k], sby.at[k], rby.at[j, k], beside[k])

    def spread_az(j, d):
        here = piece(a_block(lo, d), j)
        return remote(here, here, taz.at[d], uaz.at[j, d], back[d])

    def spread_ay(j, k):
        here = piece(a_block(lo, 0), j, 2)
        return remote(here, here, tay.at[k], uay.at[j, k], beside[k])

    def spread_by(j, k):
        here = piece(b_block(lo, turn), j)
        return remote(here, here, tby.at[k], uby.at[j, k], beside[k])

    def spread_bz(j, d):
        here = piece(b_block(0, d), j, nb)
        return remote(here, here, tbz.at[d], ubz.at[j, d], back[d])

    def on(j, condition=None):
        inside = (j >= 0) & (j < jobs)
        return pl.when(inside if condition is None else inside & condition)

    def ready(j):
        slot = lax.rem(j, slots)
        produce(j, slot)
        for k in range(side):
            ay_out[j, k] = partial[slot, pl.ds(peers[k] * 2, 2)].astype(BF16)
        for d in range(2):
            @pl.when(pos[d] == 0)
            def _(d=d):
                bz_out[j, d] = partial[slot, pl.ds(b_block(0, d), nb)].astype(BF16)

    def begin(j):
        for k in range(side):
            copy_ay(j, k).start()
        for d in range(2):
            @pl.when(pos[d] == 0)
            def _(d=d):
                copy_bz(j, d).start()

    def pair(j):
        slot = lax.rem(j, slots)
        for k in range(side):
            copy_ay(j, k).wait_recv()
        for d in range(2):
            total = partial[slot, a_block(lo, d)]
            for k in range(side):
                total = total + ay_in[j, k, d].astype(F32)
            partial[slot, a_block(lo, d)] = total

            @pl.when(pos[d] == 0)
            def _(d=d, total=total):
                az_out[j, d] = total.astype(BF16)
                copy_az(j, d).start()

    def along_a(j, d):
        slot = lax.rem(j, slots)
        copy_az(j, d).wait_recv()
        total = partial[slot, a_block(lo, d)] + az_in[j, d].astype(F32)

        @pl.when(pos[d] < na - 1)
        def _():
            az_out[j, d] = total.astype(BF16)
            copy_az(j, d).start()

        @pl.when(pos[d] == na - 1)
        def _():
            finish(j, 0, a_block(lo, d), total)
            spread_az(j, d).start()

    def along_b(j, d):
        slot = lax.rem(j, slots)
        copy_bz(j, d).wait_recv()

        @pl.when(pos[d] < na - 1)
        def _():
            for y in range(nb):
                total = partial[slot, b_block(y, d)] + bz_in[j, d, y].astype(F32)
                bz_out[j, d, y] = total.astype(BF16)
            copy_bz(j, d).start()

        @pl.when(pos[d] == na - 1)
        def _():
            for k in range(side):
                total = partial[slot, b_block(peers[k], d)]
                total = total + bz_in[j, d, peers[k]].astype(F32)
                by_out[j, k] = total.astype(BF16)
                copy_by(j, k).start()
            total = partial[slot, b_block(lo, d)] + bz_in[j, d, lo].astype(F32)
            partial[slot, b_block(lo, d)] = total

    def corner(j):
        slot = lax.rem(j, slots)
        block = b_block(lo, turn)
        total = partial[slot, block]
        for k in range(side):
            copy_by(j, k).wait_recv()
            total = total + by_in[j, k].astype(F32)
        finish(j, 1, block, total)
        for k in range(side):
            spread_by(j, k).start()

    def leave_b(j):
        for k in range(side):
            spread_by(j, k).wait_recv()
        for d in range(2):
            @pl.when(pos[d] == na - 1)
            def _(d=d):
                spread_bz(j, d).start()

    def pass_a(j, d):
        spread_az(j, d).wait_recv()

        @pl.when(far[d] < na - 1)
        def _():
            spread_az(j, d).start()

        @pl.when(far[d] > far[1 - d] - d)
        def _():
            for k in range(side):
                spread_ay(j, k).start()

    def pass_b(j, d):
        spread_bz(j, d).wait_recv()

        @pl.when(far[d] < na - 1)
        def _():
            spread_bz(j, d).start()

    start_a, walk_a, walk_b, turn_b, turn_c, open_a, open_b = steps
    top = start_a + walk_a * (na - 1)
    turn_at = walk_b * (na - 1) + turn_b
    leave_at = turn_at + turn_c
    done = 1 + max(top + open_a * na, leave_at + open_b * (na - 1))

    def tick(t, carry):
        on(t)(functools.partial(begin, t))
        j = t - start_a
        on(j)(functools.partial(pair, j))
        for d in range(2):
            j = t - walk_b * pos[d]
            on(j, pos[d] > 0)(functools.partial(along_b, j, d))
        for d in range(2):
            j = t - start_a - walk_a * pos[d]
            on(j, pos[d] > 0)(functools.partial(along_a, j, d))
        j = t - turn_at
        on(j, end)(functools.partial(corner, j))
        j = t - leave_at
        on(j, end)(functools.partial(leave_b, j))
        for d in range(2):
            j = t - top - open_a * far[d]
            on(j, far[d] > 0)(functools.partial(pass_a, j, d))
        for d in range(2):
            j = t - leave_at - open_b * far[d]
            on(j, far[d] > 0)(functools.partial(pass_b, j, d))
        on(t + 1)(functools.partial(ready, t + 1))
        j = t - done
        on(j)(functools.partial(arrive, j))
        return carry

    def arrive(j):
        for k in range(side):
            spread_ay(j, k).wait_recv()
        consume(j)

    ready(0)
    lax.fori_loop(0, jobs + done, tick, 0)

    def drain():
        def spent(block, count, send, recv, where):
            here = out.at[pl.ds(block, count)]
            remote(here, here, send, recv, where).wait_send()

        for k in range(side):
            remote(
                ay_out.at[:, k], ay_in.at[:, k], say.at[k], ray.at[0, k], beside[k]
            ).wait_send()
            spent(a_block(lo, 0), 2, tay.at[k], uay.at[0, k], beside[k])
        for d in range(2):
            @pl.when(pos[d] < na - 1)
            def _(d=d):
                remote(
                    az_out.at[:, d], az_in.at[:, d], saz.at[d], raz.at[0, d], onward[d]
                ).wait_send()
                remote(
                    bz_out.at[:, d], bz_in.at[:, d], sbz.at[d], rbz.at[0, d], onward[d]
                ).wait_send()

            @pl.when(far[d] < na - 1)
            def _(d=d):
                spent(a_block(lo, d), 1, taz.at[d], uaz.at[0, d], back[d])
                spent(b_block(0, d), nb, tbz.at[d], ubz.at[0, d], back[d])

        @pl.when(end)
        def _():
            for k in range(side):
                remote(
                    by_out.at[:, k], by_in.at[:, k], sby.at[k], rby.at[0, k], beside[k]
                ).wait_send()
                spent(b_block(lo, turn), 1, tby.at[k], uby.at[0, k], beside[k])

    return drain


def relay_scratch(dims, rows, width):
    na, nb, jobs, slots = dims
    side = max(nb - 1, 1)
    dma = pltpu.SemaphoreType.DMA

    def room(*shape):
        return pltpu.VMEM((jobs,) + shape + (rows, width), BF16)

    bufs = [
        room(side, 2), room(side, 2), room(2), room(2),
        room(2, nb), room(2, nb), room(side), room(side),
    ]
    counts = [(side,), (2,), (2,), (side,), (side,), (2,), (2,), (side,)]
    sems = [dma(lead + c) for c in counts for lead in ((), (jobs,))]
    partial = pltpu.VMEM((slots, 4 * nb, rows, width), F32)
    return [partial] + bufs + sems


def ring_slots(na, steps):
    return 2 + max(steps[0] + steps[1] * (na - 1), steps[2] * (na - 1) + steps[3])


def layout_of(tok, tokens):
    na = 4 if tok % 4 == 0 else tok
    nb = tok // na
    return na, nb, tokens // (4 * nb)


def plane(sizes):
    ngrp, nwid = sizes
    g, w = lax.axis_index("grp"), lax.axis_index("wid")
    spots = [
        ((d, e), lax.rem(g + d, ngrp), lax.rem(w + e, nwid))
        for d in range(ngrp) for e in range(nwid) if d or e
    ]
    return g * nwid + w, [(step, p * nwid + q, {"grp": p, "wid": q}) for step, p, q in spots]


def spreader(sizes, view, mine, sems):
    ngrp, nwid = sizes
    send, recv = sems
    g, w = lax.axis_index("grp"), lax.axis_index("wid")

    def copy(d, e, block, source=None):
        n = d * nwid + e - 1
        if e == 0:
            where = {"grp": lax.rem(g + d, ngrp)}
        else:
            where = {"wid": lax.rem(w + e, nwid)}
        here = view(block)
        return remote(here if source is None else source, here, send.at[n], recv.at[n], where)

    direct = [(d, 0) for d in range(1, ngrp)] + [(0, e) for e in range(1, nwid)]
    handed = [(d, e) for d in range(1, ngrp) for e in range(1, nwid)]

    def origin(d):
        return lax.rem(g + ngrp - d, ngrp) * nwid + w

    def first():
        for d, e in direct:
            copy(d, e, g * nwid + w, mine).start()

    def second():
        for d in range(1, ngrp):
            copy(d, 0, g * nwid + w).wait_recv()
        for d, e in handed:
            copy(d, e, origin(d)).start()

    def last():
        for e in range(1, nwid):
            copy(0, e, g * nwid + w).wait_recv()
        for d, e in handed:
            copy(d, e, origin(d)).wait_recv()

    def close():
        for d, e in direct + handed:
            copy(d, e, g * nwid + w).wait_send()

    return first, second, last, close


def step_kernel(dims, dims_back, counts, group, sizes, *refs):
    na, nb, jobs, slots = dims
    many = len(counts)
    x_ref = refs[0]
    weights = [refs[1 + 2 * i: 3 + 2 * i] for i in range(many)]
    downs = refs[1 + 2 * many: 1 + 3 * many]
    (
        x, turned, target, own, full, grads, out, kept, near,
        held, loaded, below, lowered, stored, total_of, shares, got,
        sx, rx, ss, rs, se, re,
    ) = refs[1 + 3 * many: 24 + 3 * many]
    rest = refs[24 + 3 * many:]
    partial, bufs, sems = rest[0], rest[1:9], rest[9:25]
    partial_back, bufs_back, sems_back = rest[25], rest[26:34], rest[34:]
    starts = [sum(counts[:i]) for i in range(many + 1)]
    rows = out.shape[1]
    kept_jobs = kept.shape[2] // (2 * LANES * group)
    near_units = starts[many - 1]
    near_job = (near_units - 1) // group
    members, height, features = full.shape[1:]
    pieces = rs.shape[0]
    step = features // pieces
    me, places = plane(sizes)

    cases = cases_of(starts, group, jobs)
    first_below = near_units // group
    depth = below.shape[0]
    side_width = group * LANES

    def between(j, low, high):
        return pl.when((j >= low) & (j < high))

    def window(at, size):
        return pl.ds(pl.multiple_of(at * LANES, LANES), size * LANES)

    def load(j):
        slot = lax.rem(j, SLOTS)
        for low, high, spans in cases:
            @between(j, low, high)
            def _(spans=spans):
                for n, u, v in spans:
                    for i in range(2):
                        pltpu.make_async_copy(
                            weights[n][i].at[:, window(j * group + u - starts[n], v - u)],
                            held.at[slot, :, pl.ds(i * side_width + u * LANES, (v - u) * LANES)],
                            loaded.at[slot],
                        ).start()

    def below_copy(j, u, v):
        slot = lax.rem(j, depth)
        return pltpu.make_async_copy(
            downs[many - 1].at[window(j * group + u - near_units, v - u), :],
            below.at[slot, pl.ds(u * LANES, (v - u) * LANES), :], lowered.at[slot],
        )

    def load_below(j):
        for low, high, spans in cases:
            for n, u, v in spans:
                if n == many - 1:
                    @between(j, low, high)
                    def _(u=u, v=v):
                        below_copy(j, u, v).start()

    def near_copy(n):
        height_n = counts[n] * LANES
        return pltpu.make_async_copy(
            downs[n], near.at[pl.ds(starts[n] * LANES, height_n), :], stored.at[n]
        )

    xs = spreader(sizes, lambda block: x.at[block], x_ref, (sx, rx))

    def share(n, p, k, block, where):
        cols = pl.ds(p * step, step)
        return remote(
            shares.at[n, block, :, cols], got.at[k, n, :, cols],
            ss.at[n, k], rs.at[p, n, k], where,
        )

    def give(n):
        for p in range(pieces):
            cols = pl.ds(p * step, step)
            shares[n, :, :, cols] = total_of[n, :, cols].astype(BF16).reshape(
                members, height, step
            )
            for k, (_, block, where) in enumerate(places):
                share(n, p, k, block, where).start()

    def prepare(barrier, count):
        for _, _, where in places:
            pl.semaphore_signal(barrier, inc=1, device_id=where, device_id_type=MESH)
        for j in range(min(SLOTS, jobs)):
            load(j)
        for n in range(many - 1):
            near_copy(n).start()
        for j in range(first_below, min(first_below + depth, jobs)):
            load_below(j)
        total_of[...] = jnp.zeros_like(total_of)
        x[me] = x_ref[...]
        pl.semaphore_wait(barrier, count + len(places))
        xs[0]()
        xs[1]()
        xs[2]()

    def produce(j, part):
        slot = lax.rem(j, SLOTS)
        left = x[...].reshape(members * height, features)
        pltpu.make_async_copy(held.at[slot], held.at[slot], loaded.at[slot]).wait()
        partial[part] = matmul(left, held[slot]).reshape(4 * nb, rows, 2 * side_width)

        @pl.when(j + SLOTS < jobs)
        def _():
            load(j + SLOTS)

    def finish(j, kind, block, total):
        gate, up = total[:, :side_width], total[:, side_width:]
        out[block, :, window(j * group, group)] = (
            gate / (1.0 + jnp.exp(-gate)) * up
        ).astype(BF16)

        @pl.when(j < kept_jobs)
        def _():
            wide = 2 * LANES * group
            kept[kind, :, pl.ds(pl.multiple_of(j * wide, LANES), wide)] = total

    def consume(j):
        for n in range(many - 1):
            pl.when(j == starts[n] // group)(lambda n=n: near_copy(n).wait())
        for low, high, spans in cases:
            @between(j, low, high)
            def _(spans=spans):
                for n, u, v in spans:
                    here = window(j * group + u, v - u)
                    left = out[:, :, here].reshape(members * height, (v - u) * LANES)
                    if n < many - 1:
                        turned[here, :] = left.T
                        right = near[here, :]
                    else:
                        below_copy(j, u, v).wait()
                        right = below[lax.rem(j, depth), pl.ds(u * LANES, (v - u) * LANES), :]
                    total_of[n] += matmul(left, right)

        @pl.when((j >= first_below) & (j + depth < jobs))
        def _():
            load_below(j + depth)

        @pl.when(j == near_job)
        def _():
            for n in range(many - 1):
                give(n)

    close = relay(
        dims, FORWARD_STEPS, produce, finish, consume, partial, out, group * LANES, bufs,
        sems, prepare,
    )

    give(many - 1)
    spreads = []
    for p in range(pieces):
        cols = pl.ds(p * step, step)
        sums = []
        for n in range(many):
            total = shares[n, me, :, cols].astype(F32)
            for k, (_, block, where) in enumerate(places):
                share(n, p, k, block, where).wait_recv()
                total = total + got[k, n, :, cols].astype(F32)
            sums.append(total)
        goal = sums[-1].astype(BF16)
        target[:, cols] = goal
        goal = goal.astype(F32)
        for n in range(many - 1):
            value = (sums[n] - goal).astype(BF16)
            own[n, :, cols] = value
            full[n, me, :, cols] = value
        spread = spreader(
            sizes, lambda block, cols=cols: full.at[:, block, :, cols], own.at[:, :, cols],
            (se.at[p], re.at[p]),
        )
        spread[0]()
        spreads.append(spread)
    for spread in spreads:
        spread[1]()
    for spread in spreads:
        spread[2]()
    close_back = backward_relay(
        dims_back, counts[:-1], group, full, near, kept, grads, partial_back, bufs_back,
        sems_back,
    )
    for spread in spreads + [xs]:
        spread[3]()
    for n in range(many):
        for k, (_, block, where) in enumerate(places):
            remote(
                shares.at[n, block], got.at[k, n], ss.at[n, k], rs.at[0, n, k], where
            ).wait_send()
    close()
    close_back()


def forward(inputs, weights, downs, tok, sizes):
    height, features = inputs.shape
    members = sizes[0] * sizes[1]
    tokens = members * height
    na, nb, rows = layout_of(tok, tokens)
    weights = [padded(w) for w in weights]
    downs = [jnp.pad(d, ((0, -d.shape[0] % LANES), (0, 0))) for d in downs]
    counts = [w.shape[1] // LANES for w in weights[::2]]
    many = len(counts)
    group = FORWARD_GROUP if sum(counts) % FORWARD_GROUP == 0 else 1
    jobs = sum(counts) // group
    dims = (na, nb, jobs, min(jobs, ring_slots(na, FORWARD_STEPS)))
    kept_jobs = -(-(sum(counts[:-1]) + BACKWARD_GROUP - 1) // group)
    width = 2 * LANES * group
    pieces = max(features // 256, 1)
    vmem = pl.BlockSpec(memory_space=pltpu.VMEM)
    hbm = pl.BlockSpec(memory_space=pltpu.HBM)
    dma = pltpu.SemaphoreType.DMA
    shape = jax.ShapeDtypeStruct
    lower = 3
    near_units = sum(counts[:-1])
    jobs_back = -(-near_units // BACKWARD_GROUP)
    dims_back = (na, nb, jobs_back, min(jobs_back, ring_slots(na, BACKWARD_STEPS)))
    outs = pl.pallas_call(
        functools.partial(step_kernel, dims, dims_back, counts, group, sizes),
        out_shape=[
            shape((members, height, features), BF16),
            shape((near_units * LANES, tokens), BF16),
            shape((height, features), BF16),
            shape((many - 1, height, features), BF16),
            shape((many - 1, members, height, features), BF16),
            shape((4 * nb, rows, jobs_back * BACKWARD_GROUP * 2 * LANES), BF16),
        ],
        in_specs=[vmem] + [hbm] * (3 * many),
        out_specs=[vmem] * 6,
        scratch_shapes=[
            pltpu.VMEM((4 * nb, rows, jobs * group * LANES), BF16),
            pltpu.VMEM((2, rows, kept_jobs * width), F32),
            pltpu.VMEM((near_units * LANES, features), BF16),
            pltpu.VMEM((SLOTS, features, width), BF16), dma((SLOTS,)),
            pltpu.VMEM((lower, group * LANES, features), BF16), dma((lower,)), dma((many - 1,)),
            pltpu.VMEM((many, tokens, features), F32),
            pltpu.VMEM((many, members, height, features), BF16),
            pltpu.VMEM((members - 1, many, height, features), BF16),
            dma((members - 1,)), dma((members - 1,)),
            dma((many, members - 1)), dma((pieces, many, members - 1)),
            dma((pieces, members - 1)), dma((pieces, members - 1)),
        ] + relay_scratch(dims, rows, width)
        + relay_scratch(dims_back, rows, BACKWARD_GROUP * LANES),
        compiler_params=pltpu.CompilerParams(
            collective_id=2, has_side_effects=True, vmem_limit_bytes=STEP_MIB * MIB
        ),
        name="distill_step",
    )(inputs, *weights, *downs)
    return outs, counts


def backward_relay(dims, counts, kept_group, full, near, kept, out, partial, bufs, sems):
    na, nb, jobs, slots = dims
    many = len(counts)
    group = BACKWARD_GROUP
    starts = [sum(counts[:i]) for i in range(many + 1)]
    rows = out.shape[1]
    features = full.shape[3]

    cases = cases_of(starts, group, jobs)

    def produce(j, part):
        for low, high, spans in cases:
            @pl.when((j >= low) & (j < high))
            def _(spans=spans):
                for n, u, v in spans:
                    error = full[n].reshape(4 * nb * rows, features)
                    row = pl.multiple_of((j * group + u) * LANES, LANES)
                    product = outer_cols(error, near[pl.ds(row, (v - u) * LANES), :])
                    partial[part, :, :, u * LANES: v * LANES] = product.reshape(
                        4 * nb, rows, (v - u) * LANES
                    )
                last = spans[-1][2]
                if last < group:
                    partial[part, :, :, last * LANES:] = jnp.zeros(
                        (4 * nb, rows, (group - last) * LANES), F32
                    )

    def finish(j, kind, block, total):
        for u in range(group):
            column = pl.multiple_of((j * group + u) * 2 * LANES, LANES)
            c = j * group + u
            where = c // kept_group * 2 * kept_group + lax.rem(c, kept_group)
            where = pl.multiple_of(where * LANES, LANES)
            gate = kept[kind, :, pl.ds(where, LANES)]
            up = kept[kind, :, pl.ds(where + kept_group * LANES, LANES)]
            value = total[:, u * LANES: (u + 1) * LANES]
            s = 1.0 / (1.0 + jnp.exp(-gate))
            out[block, :, pl.ds(column, LANES)] = (
                value * up * s * (1.0 + gate * (1.0 - s))
            ).astype(BF16)
            out[block, :, pl.ds(column + LANES, LANES)] = (value * gate * s).astype(BF16)

    return relay(
        dims, BACKWARD_STEPS, produce, finish, lambda j: None, partial, out,
        group * 2 * LANES, bufs, sems, None,
    )


def cases_of(starts, group, jobs):
    cases = []
    for j in range(jobs):
        spans = []
        for n in range(len(starts) - 1):
            low, high = max(starts[n], j * group), min(starts[n + 1], (j + 1) * group)
            if low < high:
                spans.append((n, low - j * group, high - j * group))
        if cases and cases[-1][2] == spans:
            cases[-1] = (cases[-1][0], j + 1, spans)
        else:
            cases.append((j, j + 1, spans))
    return cases


def padded(x):
    return jnp.pad(x, ((0, 0), (0, -x.shape[1] % LANES)))


def outer_kernel(counts, tile, columns, grads, turned, full, target, own, *refs):
    many = len(counts)
    total = 1 + 4 * many
    outs, stages, sems = refs[:total], refs[total: total + 3 * many], refs[-1]
    tokens, features = columns.shape

    def put(source, at):
        return pltpu.make_async_copy(source, outs[at], sems.at[at])

    put(target, 0).start()
    for n in range(many):
        put(own.at[n], 1 + n).start()
    ends = [(target, 0)] + [(own.at[n], 1 + n) for n in range(many)]

    def part(n, at, start, size):
        rows = pl.ds(start, size)
        return pltpu.make_async_copy(
            stages[n].at[rows, :], outs[at].at[rows, :], sems.at[at]
        )

    first = 1 + many
    c = 0
    for n, count in enumerate(counts):
        error = full[n].reshape(tokens, features)
        height = outs[first + n].shape[0]
        for start in range(0, height, tile):
            size = min(tile, height - start)
            at = c * LANES + start
            stages[n][start: start + size, :] = matmul(
                turned[at: at + size, :], error
            ).astype(BF16)
            part(n, first + n, start, size).start()
        ends.append((stages[n], first + n))
        c += count

    def block(i, carry):
        start = pl.multiple_of(i * tile, tile)
        rows = pl.ds(start, tile)
        left = columns[:, rows].T
        c = 0
        for n, count in enumerate(counts):
            k = many + 2 * n
            gate, up = stages[k], stages[k + 1]
            for u in range(count):
                product = matmul(left, grads[:, c * 2 * LANES: (c + 1) * 2 * LANES])
                product = product.astype(BF16)
                size = min(LANES, gate.shape[1] - u * LANES)
                gate[rows, u * LANES: u * LANES + size] = product[:, :size]
                up[rows, u * LANES: u * LANES + size] = product[:, LANES: LANES + size]
                c += 1
            part(k, first + k, start, tile).start()
            part(k + 1, first + k + 1, start, tile).start()
        return carry

    lax.fori_loop(0, features // tile, block, 0)
    for k in range(many, 3 * many):
        ends.append((stages[k], first + k))
    for source, at in ends:
        put(source, at).wait()


def weight_grads(columns, grads, turned, full, target, own, counts, widths):
    tokens, features = columns.shape
    tile = GRAD_TILE if features % GRAD_TILE == 0 else features
    many, members, height = full.shape[:3]
    out_bytes = 6 * features * sum(widths)
    shape = jax.ShapeDtypeStruct
    big = [(w, features) for w in widths] + [(features, w) for w in widths for _ in range(2)]
    small = [(height, features)] * (1 + many)
    vmem = pl.BlockSpec(memory_space=pltpu.VMEM)
    return pl.pallas_call(
        functools.partial(outer_kernel, counts, tile),
        out_shape=[shape(x, BF16) for x in small + big],
        in_specs=[vmem] * 6,
        out_specs=[pl.BlockSpec(memory_space=pltpu.HBM)] * len(small + big),
        scratch_shapes=[pltpu.VMEM(x, BF16) for x in big]
        + [pltpu.SemaphoreType.DMA((len(small + big),))],
        compiler_params=pltpu.CompilerParams(vmem_limit_bytes=40 * MIB),
        cost_estimate=pl.CostEstimate(
            flops=tokens * out_bytes, bytes_accessed=out_bytes, transcendentals=0
        ),
        name="weight_grads",
    )(columns, grads, turned, full, target, own)


def body(
    tok, sizes, inputs, parent_gate, parent_up, parent_down, first_gate, first_up, first_down,
    second_gate, second_up, second_down,
):
    weights = (first_gate, first_up, second_gate, second_up, parent_gate, parent_up)
    downs = (first_down, second_down, parent_down)
    (x, turned, target, own, full, grads), counts = forward(
        inputs, weights, downs, tok, sizes
    )
    tokens = x.shape[0] * x.shape[1]
    counts = counts[:-1]
    (
        target, first_error, second_error, first_grad_down, second_grad_down,
        first_grad_gate, first_grad_up, second_grad_gate, second_grad_up,
    ) = weight_grads(
        x.reshape(tokens, -1), grads.reshape(tokens, -1), turned, full, target, own, counts,
        [first_gate.shape[1], second_gate.shape[1]],
    )
    return (
        target, first_error, second_error,
        first_grad_gate, first_grad_up, first_grad_down,
        second_grad_gate, second_grad_up, second_grad_down,
    )


def solution(mesh):
    tok = mesh.shape["tok"]
    sizes = (mesh.shape["grp"], mesh.shape["wid"])
    rows = P(("grp", "wid"), "tok")
    cols = P("tok", ("grp", "wid"))
    return jax.shard_map(
        functools.partial(body, tok, sizes),
        mesh=mesh,
        in_specs=(rows, cols, cols, rows, cols, cols, rows, cols, cols, rows),
        out_specs=(rows, rows, rows, cols, cols, rows, cols, cols, rows),
        check_vma=False,
    )
```

```python
import functools

import jax
import jax.numpy as jnp
from jax import lax
from jax.experimental import pallas as pl
from jax.experimental.pallas import tpu as pltpu
from jax.sharding import PartitionSpec as P

MESH = pl.DeviceIdType.MESH
LANES = 128
MIB = 1024 * 1024
SLOTS = 4
FORWARD_STEPS = (3, 3, 3, 3, 3, 3, 3)
BACKWARD_STEPS = (2, 2, 2, 2, 2, 2, 2)
FORWARD_GROUP = 3
BACKWARD_GROUP = 5
STEP_MIB = 50
GRAD_TILE = 256
F32 = jnp.float32
BF16 = jnp.bfloat16


def matmul(left, right):
    return jnp.dot(left, right, preferred_element_type=F32)


def outer_cols(left, right):
    return lax.dot_general(left, right, (((1,), (1,)), ((), ())), preferred_element_type=F32)


def remote(src, dst, send, recv, where):
    return pltpu.make_async_remote_copy(
        src_ref=src, dst_ref=dst, send_sem=send, recv_sem=recv,
        device_id=where, device_id_type=MESH,
    )


def relay(dims, steps, produce, finish, consume, partial, out, span, bufs, sems, prepare):
    na, nb, jobs, slots = dims
    side = nb - 1
    ay_out, ay_in, az_out, az_in, bz_out, bz_in, by_out, by_in = bufs
    (say, ray, saz, raz, sbz, rbz, sby, rby,
     tay, uay, taz, uaz, tbz, ubz, tby, uby) = sems

    me = lax.axis_index("tok")
    hi, lo = me // nb, lax.rem(me, nb)
    peers = [lax.rem(lo + d, nb) for d in range(1, nb)]
    beside = [{"tok": hi * nb + p} for p in peers]
    pos = [hi, na - 1 - hi]
    far = [na - 1 - p for p in pos]
    onward = [
        {"tok": lax.rem(hi + 1, na) * nb + lo}, {"tok": lax.rem(hi + na - 1, na) * nb + lo}
    ]
    back = onward[::-1]
    end = (hi == 0) | (hi == na - 1)
    turn = jnp.where(hi == na - 1, 0, 1)

    if prepare is not None:
        barrier = pltpu.get_barrier_semaphore()
        for where in beside:
            pl.semaphore_signal(barrier, inc=1, device_id=where, device_id_type=MESH)
        for d in range(2):
            @pl.when(pos[d] < na - 1)
            def _(d=d):
                pl.semaphore_signal(barrier, inc=1, device_id=onward[d], device_id_type=MESH)
        prepare(barrier, side + jnp.where(end, 1, 2))

    def a_block(y, d):
        return y * 2 + d

    def b_block(y, d):
        return 2 * nb + d * nb + y

    def piece(block, j, count=1):
        return out.at[pl.ds(block, count), :, pl.ds(pl.multiple_of(j * span, LANES), span)]

    def copy_ay(j, k):
        return remote(ay_out.at[j, k], ay_in.at[j, k], say.at[k], ray.at[j, k], beside[k])

    def copy_az(j, d):
        return remote(az_out.at[j, d], az_in.at[j, d], saz.at[d], raz.at[j, d], onward[d])

    def copy_bz(j, d):
        return remote(bz_out.at[j, d], bz_in.at[j, d], sbz.at[d], rbz.at[j, d], onward[d])

    def copy_by(j, k):
        return remote(by_out.at[j, k], by_in.at[j, k], sby.at[k], rby.at[j, k], beside[k])

    def spread_az(j, d):
        here = piece(a_block(lo, d), j)
        return remote(here, here, taz.at[d], uaz.at[j, d], back[d])

    def spread_ay(j, k):
        here = piece(a_block(lo, 0), j, 2)
        return remote(here, here, tay.at[k], uay.at[j, k], beside[k])

    def spread_by(j, k):
        here = piece(b_block(lo, turn), j)
        return remote(here, here, tby.at[k], uby.at[j, k], beside[k])

    def spread_bz(j, d):
        here = piece(b_block(0, d), j, nb)
        return remote(here, here, tbz.at[d], ubz.at[j, d], back[d])

    def on(j, condition=None):
        inside = (j >= 0) & (j < jobs)
        return pl.when(inside if condition is None else inside & condition)

    def ready(j):
        slot = lax.rem(j, slots)
        produce(j, slot)
        for k in range(side):
            ay_out[j, k] = partial[slot, pl.ds(peers[k] * 2, 2)].astype(BF16)
        for d in range(2):
            @pl.when(pos[d] == 0)
            def _(d=d):
                bz_out[j, d] = partial[slot, pl.ds(b_block(0, d), nb)].astype(BF16)

    def begin(j):
        for k in range(side):
            copy_ay(j, k).start()
        for d in range(2):
            @pl.when(pos[d] == 0)
            def _(d=d):
                copy_bz(j, d).start()

    def pair(j):
        slot = lax.rem(j, slots)
        for k in range(side):
            copy_ay(j, k).wait_recv()
        for d in range(2):
            total = partial[slot, a_block(lo, d)]
            for k in range(side):
                total = total + ay_in[j, k, d].astype(F32)
            partial[slot, a_block(lo, d)] = total

            @pl.when(pos[d] == 0)
            def _(d=d, total=total):
                az_out[j, d] = total.astype(BF16)
                copy_az(j, d).start()

    def along_a(j, d):
        slot = lax.rem(j, slots)
        copy_az(j, d).wait_recv()
        total = partial[slot, a_block(lo, d)] + az_in[j, d].astype(F32)

        @pl.when(pos[d] < na - 1)
        def _():
            az_out[j, d] = total.astype(BF16)
            copy_az(j, d).start()

        @pl.when(pos[d] == na - 1)
        def _():
            finish(j, 0, a_block(lo, d), total)
            spread_az(j, d).start()

    def along_b(j, d):
        slot = lax.rem(j, slots)
        copy_bz(j, d).wait_recv()

        @pl.when(pos[d] < na - 1)
        def _():
            for y in range(nb):
                total = partial[slot, b_block(y, d)] + bz_in[j, d, y].astype(F32)
                bz_out[j, d, y] = total.astype(BF16)
            copy_bz(j, d).start()

        @pl.when(pos[d] == na - 1)
        def _():
            for k in range(side):
                total = partial[slot, b_block(peers[k], d)]
                total = total + bz_in[j, d, peers[k]].astype(F32)
                by_out[j, k] = total.astype(BF16)
                copy_by(j, k).start()
            total = partial[slot, b_block(lo, d)] + bz_in[j, d, lo].astype(F32)
            partial[slot, b_block(lo, d)] = total

    def corner(j):
        slot = lax.rem(j, slots)
        block = b_block(lo, turn)
        total = partial[slot, block]
        for k in range(side):
            copy_by(j, k).wait_recv()
            total = total + by_in[j, k].astype(F32)
        finish(j, 1, block, total)
        for k in range(side):
            spread_by(j, k).start()

    def leave_b(j):
        for k in range(side):
            spread_by(j, k).wait_recv()
        for d in range(2):
            @pl.when(pos[d] == na - 1)
            def _(d=d):
                spread_bz(j, d).start()

    def pass_a(j, d):
        spread_az(j, d).wait_recv()

        @pl.when(far[d] < na - 1)
        def _():
            spread_az(j, d).start()

        @pl.when(far[d] > far[1 - d] - d)
        def _():
            for k in range(side):
                spread_ay(j, k).start()

    def pass_b(j, d):
        spread_bz(j, d).wait_recv()

        @pl.when(far[d] < na - 1)
        def _():
            spread_bz(j, d).start()

    start_a, walk_a, walk_b, turn_b, turn_c, open_a, open_b = steps
    top = start_a + walk_a * (na - 1)
    turn_at = walk_b * (na - 1) + turn_b
    leave_at = turn_at + turn_c
    done = 1 + max(top + open_a * na, leave_at + open_b * (na - 1))

    def tick(t, carry):
        on(t)(functools.partial(begin, t))
        j = t - start_a
        on(j)(functools.partial(pair, j))
        for d in range(2):
            j = t - walk_b * pos[d]
            on(j, pos[d] > 0)(functools.partial(along_b, j, d))
        for d in range(2):
            j = t - start_a - walk_a * pos[d]
            on(j, pos[d] > 0)(functools.partial(along_a, j, d))
        j = t - turn_at
        on(j, end)(functools.partial(corner, j))
        j = t - leave_at
        on(j, end)(functools.partial(leave_b, j))
        for d in range(2):
            j = t - top - open_a * far[d]
            on(j, far[d] > 0)(functools.partial(pass_a, j, d))
        for d in range(2):
            j = t - leave_at - open_b * far[d]
            on(j, far[d] > 0)(functools.partial(pass_b, j, d))
        on(t + 1)(functools.partial(ready, t + 1))
        j = t - done
        on(j)(functools.partial(arrive, j))
        return carry

    def arrive(j):
        for k in range(side):
            spread_ay(j, k).wait_recv()
        consume(j)

    ready(0)
    lax.fori_loop(0, jobs + done, tick, 0)

    def drain():
        def spent(block, count, send, recv, where):
            here = out.at[pl.ds(block, count)]
            remote(here, here, send, recv, where).wait_send()

        for k in range(side):
            remote(
                ay_out.at[:, k], ay_in.at[:, k], say.at[k], ray.at[0, k], beside[k]
            ).wait_send()
            spent(a_block(lo, 0), 2, tay.at[k], uay.at[0, k], beside[k])
        for d in range(2):
            @pl.when(pos[d] < na - 1)
            def _(d=d):
                remote(
                    az_out.at[:, d], az_in.at[:, d], saz.at[d], raz.at[0, d], onward[d]
                ).wait_send()
                remote(
                    bz_out.at[:, d], bz_in.at[:, d], sbz.at[d], rbz.at[0, d], onward[d]
                ).wait_send()

            @pl.when(far[d] < na - 1)
            def _(d=d):
                spent(a_block(lo, d), 1, taz.at[d], uaz.at[0, d], back[d])
                spent(b_block(0, d), nb, tbz.at[d], ubz.at[0, d], back[d])

        @pl.when(end)
        def _():
            for k in range(side):
                remote(
                    by_out.at[:, k], by_in.at[:, k], sby.at[k], rby.at[0, k], beside[k]
                ).wait_send()
                spent(b_block(lo, turn), 1, tby.at[k], uby.at[0, k], beside[k])

    return drain


def relay_scratch(dims, rows, width):
    na, nb, jobs, slots = dims
    side = max(nb - 1, 1)
    dma = pltpu.SemaphoreType.DMA

    def room(*shape):
        return pltpu.VMEM((jobs,) + shape + (rows, width), BF16)

    bufs = [
        room(side, 2), room(side, 2), room(2), room(2),
        room(2, nb), room(2, nb), room(side), room(side),
    ]
    counts = [(side,), (2,), (2,), (side,), (side,), (2,), (2,), (side,)]
    sems = [dma(lead + c) for c in counts for lead in ((), (jobs,))]
    partial = pltpu.VMEM((slots, 4 * nb, rows, width), F32)
    return [partial] + bufs + sems


def ring_slots(na, steps):
    return 2 + max(steps[0] + steps[1] * (na - 1), steps[2] * (na - 1) + steps[3])


def layout_of(tok, tokens):
    na = 4 if tok % 4 == 0 else tok
    nb = tok // na
    return na, nb, tokens // (4 * nb)


def plane(sizes):
    ngrp, nwid = sizes
    g, w = lax.axis_index("grp"), lax.axis_index("wid")
    spots = [
        ((d, e), lax.rem(g + d, ngrp), lax.rem(w + e, nwid))
        for d in range(ngrp) for e in range(nwid) if d or e
    ]
    return g * nwid + w, [(step, p * nwid + q, {"grp": p, "wid": q}) for step, p, q in spots]


def spreader(sizes, view, mine, sems):
    ngrp, nwid = sizes
    send, recv = sems
    g, w = lax.axis_index("grp"), lax.axis_index("wid")

    def copy(d, e, block, source=None):
        n = d * nwid + e - 1
        if e == 0:
            where = {"grp": lax.rem(g + d, ngrp)}
        else:
            where = {"wid": lax.rem(w + e, nwid)}
        here = view(block)
        return remote(here if source is None else source, here, send.at[n], recv.at[n], where)

    direct = [(d, 0) for d in range(1, ngrp)] + [(0, e) for e in range(1, nwid)]
    handed = [(d, e) for d in range(1, ngrp) for e in range(1, nwid)]

    def origin(d):
        return lax.rem(g + ngrp - d, ngrp) * nwid + w

    def first():
        for d, e in direct:
            copy(d, e, g * nwid + w, mine).start()

    def second():
        for d in range(1, ngrp):
            copy(d, 0, g * nwid + w).wait_recv()
        for d, e in handed:
            copy(d, e, origin(d)).start()

    def last():
        for e in range(1, nwid):
            copy(0, e, g * nwid + w).wait_recv()
        for d, e in handed:
            copy(d, e, origin(d)).wait_recv()

    def close():
        for d, e in direct + handed:
            copy(d, e, g * nwid + w).wait_send()

    return first, second, last, close


def step_kernel(dims, dims_back, counts, group, sizes, *refs):
    na, nb, jobs, slots = dims
    many = len(counts)
    x_ref = refs[0]
    weights = [refs[1 + 2 * i: 3 + 2 * i] for i in range(many)]
    downs = refs[1 + 2 * many: 1 + 3 * many]
    (
        x, turned, target, own, full, grads, out, kept, near,
        held, loaded, below, lowered, stored, total_of, shares, got,
        sx, rx, ss, rs, se, re, mine,
    ) = refs[1 + 3 * many: 25 + 3 * many]
    rest = refs[25 + 3 * many:]
    partial, bufs, sems = rest[0], rest[1:9], rest[9:25]
    partial_back, bufs_back, sems_back = rest[25], rest[26:34], rest[34:]
    starts = [sum(counts[:i]) for i in range(many + 1)]
    rows = out.shape[1]
    kept_jobs = kept.shape[2] // (2 * LANES * group)
    near_units = starts[many - 1]
    near_job = (near_units - 1) // group
    members, height, features = full.shape[1:]
    pieces = rs.shape[0]
    step = features // pieces
    me, places = plane(sizes)

    cases = cases_of(starts, group, jobs)
    first_below = near_units // group
    depth = below.shape[0]
    side_width = group * LANES

    def between(j, low, high):
        return pl.when((j >= low) & (j < high))

    def window(at, size):
        return pl.ds(pl.multiple_of(at * LANES, LANES), size * LANES)

    def load(j):
        slot = lax.rem(j, SLOTS)
        for low, high, spans in cases:
            @between(j, low, high)
            def _(spans=spans):
                for n, u, v in spans:
                    for i in range(2):
                        pltpu.make_async_copy(
                            weights[n][i].at[:, window(j * group + u - starts[n], v - u)],
                            held.at[slot, :, pl.ds(i * side_width + u * LANES, (v - u) * LANES)],
                            loaded.at[slot],
                        ).start()

    def below_copy(j, u, v):
        slot = lax.rem(j, depth)
        return pltpu.make_async_copy(
            downs[many - 1].at[window(j * group + u - near_units, v - u), :],
            below.at[slot, pl.ds(u * LANES, (v - u) * LANES), :], lowered.at[slot],
        )

    def load_below(j):
        for low, high, spans in cases:
            for n, u, v in spans:
                if n == many - 1:
                    @between(j, low, high)
                    def _(u=u, v=v):
                        below_copy(j, u, v).start()

    def near_copy(n):
        height_n = counts[n] * LANES
        return pltpu.make_async_copy(
            downs[n], near.at[pl.ds(starts[n] * LANES, height_n), :], stored.at[n]
        )

    xs = spreader(sizes, lambda block: x.at[block], None, (sx, rx))
    x_own = pltpu.make_async_copy(x_ref, x.at[me], mine)

    def share(n, p, k, block, where):
        cols = pl.ds(p * step, step)
        return remote(
            shares.at[n, block, :, cols], got.at[k, n, :, cols],
            ss.at[n, k], rs.at[p, n, k], where,
        )

    def give(n):
        for p in range(pieces):
            cols = pl.ds(p * step, step)
            shares[n, :, :, cols] = total_of[n, :, cols].astype(BF16).reshape(
                members, height, step
            )
            for k, (_, block, where) in enumerate(places):
                share(n, p, k, block, where).start()

    def prepare(barrier, count):
        x_own.start()
        for _, _, where in places:
            pl.semaphore_signal(barrier, inc=1, device_id=where, device_id_type=MESH)
        for j in range(min(SLOTS, jobs)):
            load(j)
        for n in range(many - 1):
            near_copy(n).start()
        for j in range(first_below, min(first_below + depth, jobs)):
            load_below(j)
        total_of[...] = jnp.zeros_like(total_of)
        x_own.wait()
        pl.semaphore_wait(barrier, count + len(places))
        xs[0]()
        xs[1]()
        xs[2]()

    def produce(j, part):
        slot = lax.rem(j, SLOTS)
        left = x[...].reshape(members * height, features)
        pltpu.make_async_copy(held.at[slot], held.at[slot], loaded.at[slot]).wait()
        partial[part] = matmul(left, held[slot]).reshape(4 * nb, rows, 2 * side_width)

        @pl.when(j + SLOTS < jobs)
        def _():
            load(j + SLOTS)

    def finish(j, kind, block, total):
        gate, up = total[:, :side_width], total[:, side_width:]
        out[block, :, window(j * group, group)] = (
            gate / (1.0 + jnp.exp(-gate)) * up
        ).astype(BF16)

        @pl.when(j < kept_jobs)
        def _():
            wide = 2 * LANES * group
            kept[kind, :, pl.ds(pl.multiple_of(j * wide, LANES), wide)] = total

    def consume(j):
        for n in range(many - 1):
            pl.when(j == starts[n] // group)(lambda n=n: near_copy(n).wait())
        for low, high, spans in cases:
            @between(j, low, high)
            def _(spans=spans):
                for n, u, v in spans:
                    here = window(j * group + u, v - u)
                    left = out[:, :, here].reshape(members * height, (v - u) * LANES)
                    if n < many - 1:
                        turned[here, :] = left.T
                        right = near[here, :]
                    else:
                        below_copy(j, u, v).wait()
                        right = below[lax.rem(j, depth), pl.ds(u * LANES, (v - u) * LANES), :]
                    total_of[n] += matmul(left, right)

        @pl.when((j >= first_below) & (j + depth < jobs))
        def _():
            load_below(j + depth)

        @pl.when(j == near_job)
        def _():
            for n in range(many - 1):
                give(n)

    close = relay(
        dims, FORWARD_STEPS, produce, finish, consume, partial, out, group * LANES, bufs,
        sems, prepare,
    )

    give(many - 1)
    spreads = []
    for p in range(pieces):
        cols = pl.ds(p * step, step)
        sums = []
        for n in range(many):
            total = shares[n, me, :, cols].astype(F32)
            for k, (_, block, where) in enumerate(places):
                share(n, p, k, block, where).wait_recv()
                total = total + got[k, n, :, cols].astype(F32)
            sums.append(total)
        goal = sums[-1].astype(BF16)
        target[:, cols] = goal
        goal = goal.astype(F32)
        for n in range(many - 1):
            value = (sums[n] - goal).astype(BF16)
            own[n, :, cols] = value
            full[n, me, :, cols] = value
        spread = spreader(
            sizes, lambda block, cols=cols: full.at[:, block, :, cols], own.at[:, :, cols],
            (se.at[p], re.at[p]),
        )
        spread[0]()
        spreads.append(spread)
    for spread in spreads:
        spread[1]()
    for spread in spreads:
        spread[2]()
    close_back = backward_relay(
        dims_back, counts[:-1], group, full, near, kept, grads, partial_back, bufs_back,
        sems_back,
    )
    for spread in spreads + [xs]:
        spread[3]()
    for n in range(many):
        for k, (_, block, where) in enumerate(places):
            remote(
                shares.at[n, block], got.at[k, n], ss.at[n, k], rs.at[0, n, k], where
            ).wait_send()
    close()
    close_back()


def forward(inputs, weights, downs, tok, sizes):
    height, features = inputs.shape
    members = sizes[0] * sizes[1]
    tokens = members * height
    na, nb, rows = layout_of(tok, tokens)
    weights = [padded(w) for w in weights]
    downs = [jnp.pad(d, ((0, -d.shape[0] % LANES), (0, 0))) for d in downs]
    counts = [w.shape[1] // LANES for w in weights[::2]]
    many = len(counts)
    group = FORWARD_GROUP if sum(counts) % FORWARD_GROUP == 0 else 1
    jobs = sum(counts) // group
    dims = (na, nb, jobs, min(jobs, ring_slots(na, FORWARD_STEPS)))
    kept_jobs = -(-(sum(counts[:-1]) + BACKWARD_GROUP - 1) // group)
    width = 2 * LANES * group
    pieces = max(features // 256, 1)
    vmem = pl.BlockSpec(memory_space=pltpu.VMEM)
    hbm = pl.BlockSpec(memory_space=pltpu.HBM)
    dma = pltpu.SemaphoreType.DMA
    shape = jax.ShapeDtypeStruct
    lower = 3
    near_units = sum(counts[:-1])
    jobs_back = -(-near_units // BACKWARD_GROUP)
    dims_back = (na, nb, jobs_back, min(jobs_back, ring_slots(na, BACKWARD_STEPS)))
    outs = pl.pallas_call(
        functools.partial(step_kernel, dims, dims_back, counts, group, sizes),
        out_shape=[
            shape((members, height, features), BF16),
            shape((near_units * LANES, tokens), BF16),
            shape((height, features), BF16),
            shape((many - 1, height, features), BF16),
            shape((many - 1, members, height, features), BF16),
            shape((4 * nb, rows, jobs_back * BACKWARD_GROUP * 2 * LANES), BF16),
        ],
        in_specs=[hbm] * (1 + 3 * many),
        out_specs=[vmem] * 6,
        scratch_shapes=[
            pltpu.VMEM((4 * nb, rows, jobs * group * LANES), BF16),
            pltpu.VMEM((2, rows, kept_jobs * width), F32),
            pltpu.VMEM((near_units * LANES, features), BF16),
            pltpu.VMEM((SLOTS, features, width), BF16), dma((SLOTS,)),
            pltpu.VMEM((lower, group * LANES, features), BF16), dma((lower,)), dma((many - 1,)),
            pltpu.VMEM((many, tokens, features), F32),
            pltpu.VMEM((many, members, height, features), BF16),
            pltpu.VMEM((members - 1, many, height, features), BF16),
            dma((members - 1,)), dma((members - 1,)),
            dma((many, members - 1)), dma((pieces, many, members - 1)),
            dma((pieces, members - 1)), dma((pieces, members - 1)), dma,
        ] + relay_scratch(dims, rows, width)
        + relay_scratch(dims_back, rows, BACKWARD_GROUP * LANES),
        compiler_params=pltpu.CompilerParams(
            collective_id=2, has_side_effects=True, vmem_limit_bytes=STEP_MIB * MIB
        ),
        name="distill_step",
    )(inputs, *weights, *downs)
    return outs, counts


def backward_relay(dims, counts, kept_group, full, near, kept, out, partial, bufs, sems):
    na, nb, jobs, slots = dims
    many = len(counts)
    group = BACKWARD_GROUP
    starts = [sum(counts[:i]) for i in range(many + 1)]
    rows = out.shape[1]
    features = full.shape[3]

    cases = cases_of(starts, group, jobs)

    def produce(j, part):
        for low, high, spans in cases:
            @pl.when((j >= low) & (j < high))
            def _(spans=spans):
                for n, u, v in spans:
                    error = full[n].reshape(4 * nb * rows, features)
                    row = pl.multiple_of((j * group + u) * LANES, LANES)
                    product = outer_cols(error, near[pl.ds(row, (v - u) * LANES), :])
                    partial[part, :, :, u * LANES: v * LANES] = product.reshape(
                        4 * nb, rows, (v - u) * LANES
                    )
                last = spans[-1][2]
                if last < group:
                    partial[part, :, :, last * LANES:] = jnp.zeros(
                        (4 * nb, rows, (group - last) * LANES), F32
                    )

    def finish(j, kind, block, total):
        for u in range(group):
            column = pl.multiple_of((j * group + u) * 2 * LANES, LANES)
            c = j * group + u
            where = c // kept_group * 2 * kept_group + lax.rem(c, kept_group)
            where = pl.multiple_of(where * LANES, LANES)
            gate = kept[kind, :, pl.ds(where, LANES)]
            up = kept[kind, :, pl.ds(where + kept_group * LANES, LANES)]
            value = total[:, u * LANES: (u + 1) * LANES]
            s = 1.0 / (1.0 + jnp.exp(-gate))
            out[block, :, pl.ds(column, LANES)] = (
                value * up * s * (1.0 + gate * (1.0 - s))
            ).astype(BF16)
            out[block, :, pl.ds(column + LANES, LANES)] = (value * gate * s).astype(BF16)

    return relay(
        dims, BACKWARD_STEPS, produce, finish, lambda j: None, partial, out,
        group * 2 * LANES, bufs, sems, None,
    )


def cases_of(starts, group, jobs):
    cases = []
    for j in range(jobs):
        spans = []
        for n in range(len(starts) - 1):
            low, high = max(starts[n], j * group), min(starts[n + 1], (j + 1) * group)
            if low < high:
                spans.append((n, low - j * group, high - j * group))
        if cases and cases[-1][2] == spans:
            cases[-1] = (cases[-1][0], j + 1, spans)
        else:
            cases.append((j, j + 1, spans))
    return cases


def padded(x):
    return jnp.pad(x, ((0, 0), (0, -x.shape[1] % LANES)))


def outer_kernel(counts, tile, columns, grads, turned, full, target, own, *refs):
    many = len(counts)
    total = 1 + 4 * many
    outs, stages, sems = refs[:total], refs[total: total + 3 * many], refs[-1]
    tokens, features = columns.shape

    def put(source, at):
        return pltpu.make_async_copy(source, outs[at], sems.at[at])

    put(target, 0).start()
    for n in range(many):
        put(own.at[n], 1 + n).start()
    ends = [(target, 0)] + [(own.at[n], 1 + n) for n in range(many)]

    def part(n, at, start, size):
        rows = pl.ds(start, size)
        return pltpu.make_async_copy(
            stages[n].at[rows, :], outs[at].at[rows, :], sems.at[at]
        )

    first = 1 + many
    c = 0
    for n, count in enumerate(counts):
        error = full[n].reshape(tokens, features)
        height = outs[first + n].shape[0]
        for start in range(0, height, tile):
            size = min(tile, height - start)
            at = c * LANES + start
            stages[n][start: start + size, :] = matmul(
                turned[at: at + size, :], error
            ).astype(BF16)
            part(n, first + n, start, size).start()
        ends.append((stages[n], first + n))
        c += count

    def block(i, carry):
        start = pl.multiple_of(i * tile, tile)
        rows = pl.ds(start, tile)
        left = columns[:, rows].T
        c = 0
        for n, count in enumerate(counts):
            k = many + 2 * n
            gate, up = stages[k], stages[k + 1]
            for u in range(count):
                product = matmul(left, grads[:, c * 2 * LANES: (c + 1) * 2 * LANES])
                product = product.astype(BF16)
                size = min(LANES, gate.shape[1] - u * LANES)
                gate[rows, u * LANES: u * LANES + size] = product[:, :size]
                up[rows, u * LANES: u * LANES + size] = product[:, LANES: LANES + size]
                c += 1
            part(k, first + k, start, tile).start()
            part(k + 1, first + k + 1, start, tile).start()
        return carry

    lax.fori_loop(0, features // tile, block, 0)
    for k in range(many, 3 * many):
        ends.append((stages[k], first + k))
    for source, at in ends:
        put(source, at).wait()


def weight_grads(columns, grads, turned, full, target, own, counts, widths):
    tokens, features = columns.shape
    tile = GRAD_TILE if features % GRAD_TILE == 0 else features
    many, members, height = full.shape[:3]
    out_bytes = 6 * features * sum(widths)
    shape = jax.ShapeDtypeStruct
    big = [(w, features) for w in widths] + [(features, w) for w in widths for _ in range(2)]
    small = [(height, features)] * (1 + many)
    vmem = pl.BlockSpec(memory_space=pltpu.VMEM)
    return pl.pallas_call(
        functools.partial(outer_kernel, counts, tile),
        out_shape=[shape(x, BF16) for x in small + big],
        in_specs=[vmem] * 6,
        out_specs=[pl.BlockSpec(memory_space=pltpu.HBM)] * len(small + big),
        scratch_shapes=[pltpu.VMEM(x, BF16) for x in big]
        + [pltpu.SemaphoreType.DMA((len(small + big),))],
        compiler_params=pltpu.CompilerParams(vmem_limit_bytes=40 * MIB),
        cost_estimate=pl.CostEstimate(
            flops=tokens * out_bytes, bytes_accessed=out_bytes, transcendentals=0
        ),
        name="weight_grads",
    )(columns, grads, turned, full, target, own)


def body(
    tok, sizes, inputs, parent_gate, parent_up, parent_down, first_gate, first_up, first_down,
    second_gate, second_up, second_down,
):
    inputs = pltpu.with_memory_space_constraint(inputs, pltpu.HBM)
    weights = (first_gate, first_up, second_gate, second_up, parent_gate, parent_up)
    downs = (first_down, second_down, parent_down)
    (x, turned, target, own, full, grads), counts = forward(
        inputs, weights, downs, tok, sizes
    )
    tokens = x.shape[0] * x.shape[1]
    counts = counts[:-1]
    (
        target, first_error, second_error, first_grad_down, second_grad_down,
        first_grad_gate, first_grad_up, second_grad_gate, second_grad_up,
    ) = weight_grads(
        x.reshape(tokens, -1), grads.reshape(tokens, -1), turned, full, target, own, counts,
        [first_gate.shape[1], second_gate.shape[1]],
    )
    return (
        target, first_error, second_error,
        first_grad_gate, first_grad_up, first_grad_down,
        second_grad_gate, second_grad_up, second_grad_down,
    )


def solution(mesh):
    tok = mesh.shape["tok"]
    sizes = (mesh.shape["grp"], mesh.shape["wid"])
    rows = P(("grp", "wid"), "tok")
    cols = P("tok", ("grp", "wid"))
    return jax.shard_map(
        functools.partial(body, tok, sizes),
        mesh=mesh,
        in_specs=(rows, cols, cols, rows, cols, cols, rows, cols, cols, rows),
        out_specs=(rows, rows, rows, cols, cols, rows, cols, cols, rows),
        check_vma=False,
    )
```
